32 devices in a mesh: src: 16 (over z, x, core), tgt: 2 (over y).
Axes of the slice: x: 2, y: 2, z: 4, core: 2. Of those that a mesh axis runs over, the one named last changes fastest.
Arguments:
- source: bfloat16 [8192, 1024], P('src', 'tgt'), may hold values from 0 to 32, as said below
- target: bfloat16 [4096, 1024], P(('tgt', 'src')), may hold values from 0 to 32, as said below
Outputs:
- fwd_mean: float32 [8192], P('src')
- bwd_mean: float32 [4096], P('tgt')
- best_margin: float32 [4, 8192], P(None, 'src')
The draws below stay inside these ranges and needn't reach their ends.
Inputs may be any that keep to these rules, and one draw needn't show every extreme that they name: `source`: every row has a positive entry. `target`: every row has a positive entry.
All inputs are finite; a program needn't handle non-finite values.
Results may differ from the reference program's by a relative error of at most 0.0003.
Values may be sent and summed in bfloat16 or wider, within the bound.
No kernel may reach another device: no remote copies, remote signals or barrier semaphores. Data moves between devices by JAX's collectives and lax.ppermute only.
A program may use at most 64 MiB of HBM per device.

```python
import math
import jax
import jax.numpy as jnp
from jax import lax

D = 1024
K = 4
SRC_DEV = 512
S = 8192
TT = 4096
N_SRC = 16


def noise_power():
    return 16.0


def positive_noise(noise_key, count):
    values = jax.random.uniform(noise_key, (count, D), jnp.float32) ** noise_power()
    return values


def target_shape(base_key):
    key_list = jax.random.split(jax.random.fold_in(base_key, 101), 4)
    basis_rows = positive_noise(key_list[0], TT)
    partner = jax.random.randint(key_list[1], (TT,), 0, TT)
    doubled = (jax.random.randint(key_list[2], (TT,), 0, 3) == 0).astype(jnp.float32)
    weights = jax.random.uniform(key_list[3], (TT,), jnp.float32, 0.5, 1.0) * doubled
    return basis_rows + weights[:, None] * basis_rows[partner]


def finish_rows(values):
    return jnp.minimum(values, 32.0).astype(jnp.bfloat16)


def draw_target(key, part):
    return finish_rows(target_shape(key))


def draw_source(key, part):
    shaped = target_shape(key)
    key_list = jax.random.split(jax.random.fold_in(key, 211), 7)
    fresh_noise = positive_noise(key_list[0], S)
    first_match = jax.random.randint(key_list[1], (S,), 0, TT)
    second_match = jax.random.randint(key_list[2], (S,), 0, TT)
    planted = (jax.random.randint(key_list[3], (S,), 0, 2) == 0).astype(jnp.float32)
    first_weight = jax.random.uniform(key_list[4], (S,), jnp.float32, 0.6, 1.2) * planted
    second_weight = jax.random.uniform(key_list[5], (S,), jnp.float32, 0.0, 0.6) * planted
    noise_weight = planted * jax.random.uniform(key_list[6], (S,), jnp.float32, 0.4, 1.2) + (1.0 - planted)
    values = first_weight[:, None] * shaped[first_match] + second_weight[:, None] * shaped[second_match]
    values = values + noise_weight[:, None] * fresh_noise
    return finish_rows(values)


def setup_inputs(seed: int = 0) -> dict:
    streams_of = jax.random.split(jax.random.key(seed), 3)
    return {
        "source": draw_source(jax.random.fold_in(streams_of[2], 71), 0),
        "target": draw_target(jax.random.fold_in(streams_of[2], 71), 0),
    }


def inverse_norm(embedded):
    values = embedded.astype(jnp.float32)
    return lax.rsqrt(lax.optimization_barrier(jnp.mean(values * values, axis=1)) + 1e-06) / math.sqrt(values.shape[1])

def top_lists(matrix, axis):
    position = lax.broadcasted_iota(jnp.int32, matrix.shape, axis)
    beyond = jnp.int32(matrix.shape[axis])
    current = matrix
    highest = []
    for turn in range(K):
        peak = lax.optimization_barrier(jnp.max(current, axis=axis, keepdims=True))
        first = lax.optimization_barrier(jnp.min(jnp.where(current == peak, position, beyond), axis=axis, keepdims=True))
        highest.append(peak)
        current = jnp.where(position == first, -jnp.inf, current)
    return jnp.concatenate(highest, axis=axis)

def reference(source, target):
    inv_src = inverse_norm(source)
    inv_tgt = inverse_norm(target)
    src_blocks = source.reshape(N_SRC, SRC_DEV, D)
    inv_blocks = inv_src.reshape(N_SRC, SRC_DEV)

    def cosines(src_block, inv_block):
        products = jnp.dot(src_block, target.T, preferred_element_type=jnp.float32)
        return products * inv_block[:, None] * inv_tgt[None, :]

    def first_pass(col_carry, block_pair):
        src_block, inv_block = block_pair
        cosine_tile = cosines(src_block, inv_block)
        row_top = top_lists(cosine_tile, 1)
        col_top = top_lists(cosine_tile, 0)
        merged = top_lists(jnp.concatenate([col_carry, col_top], axis=0), 0)
        return (merged, lax.optimization_barrier(jnp.mean(row_top, axis=1)))
    initial = jnp.full((K, TT), -10.0, dtype=jnp.float32)
    col_best, row_means = lax.scan(first_pass, initial, (src_blocks, inv_blocks))
    fwd_mean = row_means.reshape(S)
    bwd_mean = lax.optimization_barrier(jnp.mean(col_best, axis=0))
    fwd_blocks = fwd_mean.reshape(N_SRC, SRC_DEV)

    def second_pass(triple):
        src_block, inv_block, fwd_block = triple
        cosine_tile = cosines(src_block, inv_block)
        margin = cosine_tile / ((fwd_block[:, None] + bwd_mean[None, :]) * 0.5)
        return top_lists(margin, 1)
    best_lists = lax.map(second_pass, (src_blocks, inv_blocks, fwd_blocks))
    best_margin = best_lists.reshape(S, K).T
    return (fwd_mean, bwd_mean, best_margin)
```

```python
import math

import jax
import jax.numpy as jnp
from jax import lax
from jax.experimental import pallas as pl
from jax.experimental.pallas import tpu as pltpu
from jax.sharding import PartitionSpec as P

K = 4
LANES = 128
SUBLANES = 8


def bits_below(size):
    return [1 << bit for bit in range(size.bit_length() - 1)]


def exchange(values, upper, lower):
    high = jnp.maximum(values[upper], values[lower])
    values[lower] = jnp.minimum(values[upper], values[lower])
    values[upper] = high


def sort_list(values):
    values = list(values)
    for upper, lower in ((0, 1), (2, 3), (0, 2), (1, 3), (1, 2)):
        exchange(values, upper, lower)
    return values


def merge_lists(one, other):
    values = [jnp.maximum(one[k], other[K - 1 - k]) for k in range(K)]
    for upper, lower in ((0, 2), (1, 3), (0, 1), (2, 3)):
        exchange(values, upper, lower)
    return values


def reduce_lists(lists):
    while len(lists) > 1:
        merged = [merge_lists(lists[n], lists[n + 1]) for n in range(0, len(lists) - 1, 2)]
        lists = merged + lists[len(lists) - len(lists) % 2 :]
    return lists[0]


def fold(tile):
    parts = [tile[r : r + SUBLANES] for r in range(0, tile.shape[0], SUBLANES)]
    return reduce_lists([sort_list(parts[n : n + K]) for n in range(0, len(parts), K)])


def fold_sublanes(values):
    shift = SUBLANES // 2
    while shift:
        values = merge_lists(values, [pltpu.roll(v, shift, 0) for v in values])
        shift //= 2
    return values


def store_lists(ref, values, first):
    for k in range(K):
        for n in range(values[k].shape[1] // LANES):
            ref[k, first + n : first + n + 1, :] = values[k][0:1, n * LANES : (n + 1) * LANES]


def inverse_norms(rows, width):
    values = rows.astype(jnp.float32)
    total = jnp.sum(values * values, axis=1, keepdims=True)
    return lax.rsqrt(total / width + 1e-06) / math.sqrt(width)


def cosine_kernel(plan, *refs):
    n_in = sum(len(piece) for piece in plan["source"]) + len(plan["target"])
    given = refs[:n_in]
    cos_ref, row_ref, col_ref, src, tgt, sems = refs[n_in:]
    width = src.shape[1]
    mine = lax.axis_index("tgt")
    copies = []
    n = 0
    for piece in plan["source"]:
        for first, offset, rows in piece:
            feats = given[n].shape[1]
            place = pl.ds(pl.multiple_of((mine ^ offset) * feats, LANES), feats)
            copies.append(
                pltpu.make_async_copy(given[n], src.at[pl.ds(first, rows), place], sems.at[n])
            )
            n += 1
    for first, rows in plan["target"]:
        copies.append(pltpu.make_async_copy(given[n], tgt.at[pl.ds(first, rows)], sems.at[n]))
        n += 1
    for copy in copies:
        copy.start()
    for copy in copies:
        copy.wait()
    n_src, n_tgt = src.shape[0], tgt.shape[0]
    src_step = min(512, n_src)
    inv_src = []
    for first in range(0, n_src, LANES):
        inv = inverse_norms(src[first : first + LANES], width)
        inv_src.append(jnp.broadcast_to(inv, (LANES, LANES)).T[0:SUBLANES])
    row_lists = [None] * (n_src // LANES)
    for t in range(0, n_tgt, LANES):
        inv_tgt = jnp.broadcast_to(inverse_norms(tgt[t : t + LANES], width), (LANES, LANES))
        col_lists = []
        for s in range(0, n_src, src_step):
            products = lax.dot_general(
                tgt[t : t + LANES],
                src[s : s + src_step],
                (((1,), (1,)), ((), ())),
                preferred_element_type=jnp.float32,
            )
            for lane in range(0, src_step, LANES):
                block = (s + lane) // LANES
                scale = jnp.broadcast_to(inv_src[block][0:1], (LANES, LANES))
                tile = products[:, lane : lane + LANES] * scale * inv_tgt
                cos_ref[t : t + LANES, s + lane : s + lane + LANES] = tile
                found = fold(tile)
                if row_lists[block] is not None:
                    found = merge_lists(row_lists[block], found)
                row_lists[block] = found
                col_lists.append(fold(tile.T))
        store_lists(col_ref, fold_sublanes(reduce_lists(col_lists)), t // LANES)
    for block, values in enumerate(row_lists):
        store_lists(row_ref, fold_sublanes(values), block)


def margin_kernel(cos_ref, fwd_ref, bwd_ref, out_ref):
    n_tgt, n_src = cos_ref.shape
    for s in range(0, n_src, LANES):
        block = s // LANES
        fwd = jnp.broadcast_to(fwd_ref[block : block + 1, :] * 0.5, (LANES, LANES))
        lists = []
        for t in range(0, n_tgt, LANES):
            row = t // LANES
            bwd = jnp.broadcast_to(bwd_ref[row : row + 1, :] * 0.5, (LANES, LANES)).T
            lists.append(fold(cos_ref[t : t + LANES, s : s + LANES] / (fwd + bwd)))
        store_lists(out_ref, fold_sublanes(reduce_lists(lists)), block)


def in_vmem(count):
    return [pl.BlockSpec(memory_space=pltpu.VMEM)] * count


def xor_pairs(size, mask):
    return [(i, i ^ mask) for i in range(size)]


def merge_arrays(one, other):
    return jnp.stack(merge_lists([one[k] for k in range(K)], [other[k] for k in range(K)]))


def flip(array, axis, mask):
    shape = array.shape
    split = shape[:axis] + (shape[axis] // (2 * mask), 2, mask) + shape[axis + 1 :]
    parts = array.reshape(split)
    low = lax.slice_in_dim(parts, 0, 1, axis=axis + 1)
    high = lax.slice_in_dim(parts, 1, 2, axis=axis + 1)
    return jnp.concatenate([high, low], axis=axis + 1).reshape(shape)


def flip_where(bit, array, axis, mask):
    return jnp.where(bit != 0, flip(array, axis, mask), array)


def solution(mesh):
    n_src, n_tgt = mesh.shape["src"], mesh.shape["tgt"]
    near = 1 << (((n_src // 2).bit_length() - 1) // 2)
    far = n_src // 2 // near

    def over_src(array, mask):
        return lax.ppermute(array, "src", xor_pairs(n_src, mask))

    def over_tgt(array, mask):
        return lax.ppermute(array, "tgt", xor_pairs(n_tgt, mask))

    def over_both(array, src_mask, tgt_mask):
        pairs = xor_pairs(n_src * n_tgt, src_mask * n_tgt + tgt_mask)
        return lax.ppermute(array, ("src", "tgt"), pairs)

    def local(source, target):
        rows, feats = source.shape
        t_rows, width = target.shape
        at = lax.axis_index("src")
        pieces = {(0, 0): [source]}
        for b in range(near):
            for t in range(n_tgt):
                if (b, t) == (0, 0):
                    continue
                if b and t and (near, n_tgt) == (2, 2):
                    continue
                pieces[b, t] = [over_both(source, 2 * b, t)]
        if (near, n_tgt) == (2, 2):
            half = rows // 2
            pieces[1, 1] = [
                over_src(pieces[0, 1][0][:half], 2),
                over_tgt(pieces[1, 0][0][half:], 1),
            ]
        held = [target if a == 0 else over_src(target, 2 * near * a) for a in range(far)]
        given, plan = [], {"source": [], "target": []}
        for (b, t), parts in sorted(pieces.items()):
            first = b * rows
            plan["source"].append([])
            for part in parts:
                plan["source"][-1].append((first, t, part.shape[0]))
                given.append(part)
                first += part.shape[0]
        for a in range(far):
            for c in range(2):
                plan["target"].append(((2 * a + c) * t_rows, t_rows))
                given.append(held[a] if c == 0 else over_src(held[a], 1))
        block_src, block_tgt = near * rows, 2 * far * t_rows
        src_lines, tgt_lines = block_src // LANES, block_tgt // LANES
        cosines, row_best, col_best = pl.pallas_call(
            lambda *refs: cosine_kernel(plan, *refs),
            out_shape=(
                jax.ShapeDtypeStruct((block_tgt, block_src), jnp.float32),
                jax.ShapeDtypeStruct((K, src_lines, LANES), jnp.float32),
                jax.ShapeDtypeStruct((K, tgt_lines, LANES), jnp.float32),
            ),
            in_specs=[pl.BlockSpec(memory_space=pl.ANY)] * len(given),
            out_specs=tuple(in_vmem(3)),
            scratch_shapes=[
                pltpu.VMEM((block_src, width), jnp.bfloat16),
                pltpu.VMEM((block_tgt, width), jnp.bfloat16),
                pltpu.SemaphoreType.DMA((len(given),)),
            ],
            name="cosine_lists",
        )(*given)

        def line_flip(array, slots, mask):
            shaped = array.reshape(K, slots, -1)
            return flip(shaped, 1, mask).reshape(array.shape)

        col_best = merge_arrays(col_best, line_flip(over_src(col_best, 1), 2 * far, 1))
        for bit in bits_below(near):
            row_best = merge_arrays(row_best, line_flip(over_src(row_best, 2 * bit), near, bit))
        for bit in bits_below(far):
            arrived = over_src(col_best, 2 * near * bit)
            col_best = merge_arrays(col_best, line_flip(arrived, 2 * far, 2 * bit))
        for bit in bits_below(n_tgt):
            row_best = merge_arrays(row_best, over_tgt(row_best, bit))
        fwd = jnp.sum(row_best, axis=0) / K
        bwd = jnp.sum(col_best, axis=0) / K
        margins = pl.pallas_call(
            margin_kernel,
            out_shape=jax.ShapeDtypeStruct((K, src_lines, LANES), jnp.float32),
            in_specs=in_vmem(3),
            out_specs=in_vmem(1)[0],
            name="margin_lists",
        )(cosines, fwd, bwd)
        best = margins.reshape(K, near, rows // LANES, LANES)
        known = bwd.reshape(1, tgt_lines, LANES)
        kept = list(range(near))
        for bit in bits_below(near):
            send = [n for n, slot in enumerate(kept) if slot & bit]
            keep = [n for n, slot in enumerate(kept) if not slot & bit]
            lists = jnp.concatenate([best[:, n : n + 1] for n in send], axis=1)
            split = lists.size // LANES
            payload = jnp.concatenate(
                [lists.reshape(split, LANES), known.reshape(-1, LANES)], axis=0
            )
            arrived = over_src(payload, 2 * bit)
            mine = jnp.concatenate([best[:, n : n + 1] for n in keep], axis=1)
            best = merge_arrays(mine, arrived[:split].reshape(mine.shape))
            known = jnp.concatenate([known, arrived[split:].reshape(known.shape)], axis=0)
            kept = [kept[n] for n in keep]
        best = best.reshape(K, rows // LANES, LANES)
        for bit in bits_below(n_tgt):
            best = merge_arrays(best, over_tgt(best, bit))
        known = known.reshape(near, far, 2, t_rows)
        for axis, size, unit in ((0, near, 2), (1, far, 2 * near), (2, 2, 1)):
            for bit in bits_below(size):
                known = flip_where(at & (unit * bit), known, axis, bit)
        bwd_mean = known.transpose(1, 0, 2, 3).reshape(-1)
        return fwd[: rows // LANES].reshape(-1), bwd_mean, best.reshape(K, rows)

    in_specs = (P("src", "tgt"), P(("tgt", "src"), None))
    out_specs = (P("src"), P("tgt"), P(None, "src"))
    return jax.shard_map(local, mesh=mesh, in_specs=in_specs, out_specs=out_specs, check_vma=False)
```

```python
import math

import jax
import jax.numpy as jnp
from jax import lax
from jax.experimental import pallas as pl
from jax.experimental.pallas import tpu as pltpu
from jax.sharding import PartitionSpec as P

K = 4
LANES = 128
SUBLANES = 8


def bits_below(size):
    return [1 << bit for bit in range(size.bit_length() - 1)]


def exchange(values, upper, lower):
    high = jnp.maximum(values[upper], values[lower])
    values[lower] = jnp.minimum(values[upper], values[lower])
    values[upper] = high


def sort_list(values):
    values = list(values)
    for upper, lower in ((0, 1), (2, 3), (0, 2), (1, 3), (1, 2)):
        exchange(values, upper, lower)
    return values


def merge_lists(one, other):
    values = [jnp.maximum(one[k], other[K - 1 - k]) for k in range(K)]
    for upper, lower in ((0, 2), (1, 3), (0, 1), (2, 3)):
        exchange(values, upper, lower)
    return values


def reduce_lists(lists):
    while len(lists) > 1:
        merged = [merge_lists(lists[n], lists[n + 1]) for n in range(0, len(lists) - 1, 2)]
        lists = merged + lists[len(lists) - len(lists) % 2 :]
    return lists[0]


def fold(tile):
    parts = [tile[r : r + SUBLANES] for r in range(0, tile.shape[0], SUBLANES)]
    return reduce_lists([sort_list(parts[n : n + K]) for n in range(0, len(parts), K)])


def fold_sublanes(values):
    shift = SUBLANES // 2
    while shift:
        values = merge_lists(values, [pltpu.roll(v, shift, 0) for v in values])
        shift //= 2
    return values


def store_lists(ref, values, first):
    for k in range(K):
        for n in range(values[k].shape[1] // LANES):
            ref[k, first + n : first + n + 1, :] = values[k][0:1, n * LANES : (n + 1) * LANES]


def inverse_norms(rows):
    width = rows.shape[1]
    values = rows.astype(jnp.float32)
    total = jnp.sum(values * values, axis=1, keepdims=True)
    inverse = lax.rsqrt(total / width + 1e-06) / math.sqrt(width)
    return jnp.broadcast_to(inverse, (rows.shape[0], LANES))


def turn(tile):
    return jnp.concatenate(
        [tile[r : r + LANES].T for r in range(0, tile.shape[0], LANES)], axis=1
    )


def features(ref, groups, rows=slice(None)):
    mine = lax.axis_index("tgt")
    size = ref.shape[1] // groups
    places = [pl.ds(pl.multiple_of((mine ^ t) * size, LANES), size) for t in range(groups)]
    return jnp.concatenate([ref[rows, place] for place in places], axis=1)


def source_rows(piece, first, count):
    columns = []
    for parts in piece:
        at, found = 0, []
        for part in parts:
            low, high = max(first, at), min(first + count, at + part.shape[0])
            if low < high:
                found.append(part[low - at : high - at, :])
            at += part.shape[0]
        columns.append(jnp.concatenate(found, axis=0))
    return jnp.concatenate(columns, axis=1)


def cosine_block(pieces, targets, inv_src, inv_tgt, cos_ref, rows, cols, work):
    groups = len(pieces[0])
    lhs = jnp.concatenate([features(ref, groups) for ref in targets], axis=0)
    n_tgt = lhs.shape[0]
    step = 2 * LANES
    first = 0
    for b, piece in enumerate(pieces):
        n_rows = sum(part.shape[0] for part in piece[0])
        for n in range(0, n_rows, step):
            rhs = source_rows(piece, n, step)
            if inv_src[0] is None:
                inverse = turn(inverse_norms(rhs))[0:SUBLANES]
                inv_src[1][:, n : n + step] = inverse
            work[:, first : first + step] = lax.dot_general(
                lhs, rhs, (((1,), (1,)), ((), ())), preferred_element_type=jnp.float32
            )
            first += step
    if inv_tgt[0] is None:
        inv_tgt[1][...] = inverse_norms(lhs)
    inv_t = inv_tgt[0] if inv_tgt[0] is not None else inv_tgt[1]
    col_lists = [[] for _ in range(0, n_tgt, LANES)]
    first = 0
    for b, piece in enumerate(pieces):
        n_rows = sum(part.shape[0] for part in piece[0])
        inv_s = inv_src[0][b] if inv_src[0] is not None else inv_src[1]
        for n in range(0, n_rows, LANES):
            scale = jnp.broadcast_to(inv_s[0:1, n : n + LANES], (LANES, LANES))
            row_lists = []
            if rows[0] is not None:
                row_lists.append([rows[0][b][k, :, n : n + LANES] for k in range(K)])
            for t in range(0, n_tgt, LANES):
                tile = work[t : t + LANES, first : first + LANES] * scale * inv_t[t : t + LANES]
                cos_ref[t : t + LANES, first : first + LANES] = tile
                row_lists.append(fold(tile))
                col_lists[t // LANES].append(fold(tile.T))
            rows[1](b, n, reduce_lists(row_lists))
            first += LANES
    for line, lists in enumerate(col_lists):
        if cols[0] is not None:
            place = slice(line * LANES, (line + 1) * LANES)
            lists.append([cols[0][k, :, place] for k in range(K)])
        cols[1](line, reduce_lists(lists))


def store_running(ref):
    def store(*at):
        *place, values = at
        first = place[-1] if len(place) > 1 else place[0] * LANES
        for k in range(K):
            ref[k, :, first : first + LANES] = values[k]

    return store


def first_kernel(piece, targets, cos_ref, inv_src, inv_tgt, rows, cols, work):
    cosine_block(
        [piece], targets, (None, inv_src), (None, inv_tgt), cos_ref,
        (None, store_running(rows)), (None, store_running(cols)), work,
    )


def next_kernel(piece, targets, inv_tgt, cols_in, cos_ref, inv_src, rows, cols, work):
    cosine_block(
        [piece], targets, (None, inv_src), (inv_tgt, None), cos_ref,
        (None, store_running(rows)), (cols_in, store_running(cols)), work,
    )


def last_kernel(pieces, targets, inv_src, rows_in, cols_in, cos_ref, row_ref, col_ref, work, inv_tgt):
    lines = cols_in.shape[2] // LANES
    slot = rows_in[0].shape[2] // LANES

    def store_row(b, n, values):
        store_lists(row_ref, fold_sublanes(values), b * slot + n // LANES)

    def store_col(line, values):
        store_lists(col_ref, fold_sublanes(values), lines + line)

    cosine_block(
        pieces, targets, (inv_src, None), (None, inv_tgt), cos_ref,
        (rows_in, store_row), (None, store_col), work,
    )
    for line in range(lines):
        place = slice(line * LANES, (line + 1) * LANES)
        store_lists(col_ref, fold_sublanes([cols_in[k, :, place] for k in range(K)]), line)


def half_mean(ref, line):
    total = ref[0, line : line + 1, :]
    for k in range(1, K):
        total = total + ref[k, line : line + 1, :]
    return jnp.broadcast_to(total / K * 0.5, (LANES, LANES))


def margin_kernel(early, late, rows, cols, out_ref, bwd_ref):
    n_early, slot = early[0].shape
    n_late, n_src = late.shape
    for t in range(0, n_early + n_late, LANES):
        bwd_ref[t : t + LANES, :] = half_mean(cols, t // LANES).T
    for s in range(0, n_src, LANES):
        fwd = half_mean(rows, s // LANES)
        lists = []
        for t in range(0, n_early + n_late, LANES):
            if t < n_early:
                tile = early[s // slot][t : t + LANES, s % slot : s % slot + LANES]
            else:
                tile = late[t - n_early : t - n_early + LANES, s : s + LANES]
            lists.append(fold(tile / (fwd + bwd_ref[t : t + LANES, :])))
        store_lists(out_ref, fold_sublanes(reduce_lists(lists)), s // LANES)


def call(kernel, name, args, out_shapes, scratch):
    spec = pl.BlockSpec(memory_space=pltpu.VMEM)
    return pl.pallas_call(
        kernel,
        out_shape=tuple(jax.ShapeDtypeStruct(shape, jnp.float32) for shape in out_shapes),
        in_specs=jax.tree.map(lambda _: spec, list(args)),
        out_specs=tuple(spec for _ in out_shapes),
        scratch_shapes=[pltpu.VMEM(shape, jnp.float32) for shape in scratch],
        compiler_params=pltpu.CompilerParams(vmem_limit_bytes=16 << 20),
        name=name,
    )(*args)


def xor_pairs(size, mask):
    return [(i, i ^ mask) for i in range(size)]


def merge_arrays(one, other):
    return jnp.stack(merge_lists([one[k] for k in range(K)], [other[k] for k in range(K)]))


def flip(array, axis, mask):
    shape = array.shape
    split = shape[:axis] + (shape[axis] // (2 * mask), 2, mask) + shape[axis + 1 :]
    parts = array.reshape(split)
    low = lax.slice_in_dim(parts, 0, 1, axis=axis + 1)
    high = lax.slice_in_dim(parts, 1, 2, axis=axis + 1)
    return jnp.concatenate([high, low], axis=axis + 1).reshape(shape)


def flip_where(bit, array, axis, mask):
    return jnp.where(bit != 0, flip(array, axis, mask), array)


def solution(mesh):
    n_src, n_tgt = mesh.shape["src"], mesh.shape["tgt"]
    near = 1 << (((n_src // 2).bit_length() - 1) // 2)
    far = n_src // 2 // near

    def over_src(array, mask):
        return lax.ppermute(array, "src", xor_pairs(n_src, mask))

    def over_tgt(array, mask):
        return lax.ppermute(array, "tgt", xor_pairs(n_tgt, mask))

    def over_both(array, src_mask, tgt_mask):
        pairs = xor_pairs(n_src * n_tgt, src_mask * n_tgt + tgt_mask)
        return lax.ppermute(array, ("src", "tgt"), pairs)

    def local(source, target):
        rows, feats = source.shape
        t_rows, width = target.shape
        at = lax.axis_index("src")
        pieces = [[None] * n_tgt for _ in range(near)]
        square = (near, n_tgt) == (2, 2)
        held = [target] + [None] * (far - 1)
        for t in range(n_tgt):
            for b in range(near):
                if (b, t) == (0, 0):
                    pieces[b][t] = [source]
                elif not (square and b and t):
                    with jax.named_scope(f"source_{b}_{t}"):
                        pieces[b][t] = [over_both(source, 2 * b, t)]
        for a in range(1, far):
            if (far, a) != (4, 3):
                with jax.named_scope(f"target_{a}"):
                    held[a] = over_src(target, 2 * near * a)
        if square:
            half = rows // 2
            with jax.named_scope("source_1_1_near"):
                low = over_src(pieces[0][1][0][:half], 2)
            with jax.named_scope("source_1_1_tgt"):
                high = over_tgt(pieces[1][0][0][half:], 1)
            pieces[1][1] = [low, high]
        if far == 4:
            with jax.named_scope("target_3"):
                held[3] = over_src(held[2], 2 * near)
        pairs = []
        for a in range(far):
            with jax.named_scope(f"core_{a}"):
                pairs.append([held[a], over_src(held[a], 1)])
        n_late = max(1, LANES // (2 * t_rows))
        early = sum(pairs[: far - n_late], [])
        late = sum(pairs[far - n_late :], [])
        e_rows, l_rows = len(early) * t_rows, len(late) * t_rows
        block_src, block_tgt = near * rows, 2 * far * t_rows
        src_lines, tgt_lines = block_src // LANES, block_tgt // LANES
        running = (K, SUBLANES, rows), (K, SUBLANES, e_rows)
        cos, inv, inv_tgt, row_run, cols = call(
            first_kernel, "cosines_first", (pieces[0], early),
            [(e_rows, rows), (SUBLANES, rows), (e_rows, LANES), *running],
            [(e_rows, rows)],
        )
        cosines, inverses, row_runs = [cos], [inv], [row_run]
        for b in range(1, near):
            cos, inv, row_run, cols = call(
                next_kernel, f"cosines_next_{b}", (pieces[b], early, inv_tgt, cols),
                [(e_rows, rows), (SUBLANES, rows), *running],
                [(e_rows, rows)],
            )
            cosines.append(cos)
            inverses.append(inv)
            row_runs.append(row_run)
        cos_late, row_best, col_best = call(
            last_kernel, "cosines_last", (pieces, late, inverses, row_runs, cols),
            [(l_rows, block_src), (K, src_lines, LANES), (K, tgt_lines, LANES)],
            [(l_rows, block_src), (l_rows, LANES)],
        )

        def line_flip(array, slots, mask):
            shaped = array.reshape(K, slots, -1)
            return flip(shaped, 1, mask).reshape(array.shape)

        col_best = merge_arrays(col_best, line_flip(over_src(col_best, 1), 2 * far, 1))
        for bit in bits_below(near):
            row_best = merge_arrays(row_best, line_flip(over_src(row_best, 2 * bit), near, bit))
        for bit in bits_below(far):
            arrived = over_src(col_best, 2 * near * bit)
            col_best = merge_arrays(col_best, line_flip(arrived, 2 * far, 2 * bit))
        for bit in bits_below(n_tgt):
            row_best = merge_arrays(row_best, over_tgt(row_best, bit))
        (margins,) = call(
            margin_kernel, "margin_lists", (cosines, cos_late, row_best, col_best),
            [(K, src_lines, LANES)],
            [(block_tgt, LANES)],
        )
        fwd = jnp.sum(row_best, axis=0) / K
        bwd = jnp.sum(col_best, axis=0) / K
        best = margins.reshape(K, near, rows // LANES, LANES)
        known = bwd.reshape(1, tgt_lines, LANES)
        kept = list(range(near))
        for bit in bits_below(near):
            send = [n for n, slot in enumerate(kept) if slot & bit]
            keep = [n for n, slot in enumerate(kept) if not slot & bit]
            lists = jnp.concatenate([best[:, n : n + 1] for n in send], axis=1)
            split = lists.size // LANES
            payload = jnp.concatenate(
                [lists.reshape(split, LANES), known.reshape(-1, LANES)], axis=0
            )
            arrived = over_src(payload, 2 * bit)
            mine = jnp.concatenate([best[:, n : n + 1] for n in keep], axis=1)
            best = merge_arrays(mine, arrived[:split].reshape(mine.shape))
            known = jnp.concatenate([known, arrived[split:].reshape(known.shape)], axis=0)
            kept = [kept[n] for n in keep]
        best = best.reshape(K, rows // LANES, LANES)
        for bit in bits_below(n_tgt):
            best = merge_arrays(best, over_tgt(best, bit))
        known = known.reshape(near, far, 2, t_rows)
        for axis, size, unit in ((0, near, 2), (1, far, 2 * near), (2, 2, 1)):
            for bit in bits_below(size):
                known = flip_where(at & (unit * bit), known, axis, bit)
        bwd_mean = known.transpose(1, 0, 2, 3).reshape(-1)
        return fwd[: rows // LANES].reshape(-1), bwd_mean, best.reshape(K, rows)

    in_specs = (P("src", "tgt"), P(("tgt", "src"), None))
    out_specs = (P("src"), P("tgt"), P(None, "src"))
    return jax.shard_map(local, mesh=mesh, in_specs=in_specs, out_specs=out_specs, check_vma=False)
```

```python
import functools
import math

import jax
import jax.numpy as jnp
from jax import lax
from jax.experimental import pallas as pl
from jax.experimental.pallas import tpu as pltpu
from jax.sharding import PartitionSpec as P

K = 4
LANES = 128
SUBLANES = 8


def bits_below(size):
    return [1 << bit for bit in range(size.bit_length() - 1)]


def exchange(values, upper, lower):
    high = jnp.maximum(values[upper], values[lower])
    values[lower] = jnp.minimum(values[upper], values[lower])
    values[upper] = high


def sort_list(values):
    values = list(values)
    for upper, lower in ((0, 1), (2, 3), (0, 2), (1, 3), (1, 2)):
        exchange(values, upper, lower)
    return values


def merge_lists(one, other):
    values = [jnp.maximum(one[k], other[K - 1 - k]) for k in range(K)]
    for upper, lower in ((0, 2), (1, 3), (0, 1), (2, 3)):
        exchange(values, upper, lower)
    return values


def reduce_lists(lists):
    while len(lists) > 1:
        merged = [merge_lists(lists[n], lists[n + 1]) for n in range(0, len(lists) - 1, 2)]
        lists = merged + lists[len(lists) - len(lists) % 2 :]
    return lists[0]


def fold(tile):
    parts = [tile[r : r + SUBLANES] for r in range(0, tile.shape[0], SUBLANES)]
    return reduce_lists([sort_list(parts[n : n + K]) for n in range(0, len(parts), K)])


def fold_sublanes(values):
    shift = SUBLANES // 2
    while shift:
        values = merge_lists(values, [pltpu.roll(v, shift, 0) for v in values])
        shift //= 2
    return values


def store_lists(ref, values, first):
    for k in range(K):
        for n in range(values[k].shape[1] // LANES):
            ref[k, first + n : first + n + 1, :] = values[k][0:1, n * LANES : (n + 1) * LANES]


def inverse_norms(rows):
    width = rows.shape[1]
    values = rows.astype(jnp.float32)
    total = jnp.sum(values * values, axis=1, keepdims=True)
    inverse = lax.rsqrt(total / width + 1e-06) / math.sqrt(width)
    return jnp.broadcast_to(inverse, (rows.shape[0], LANES))


def turn(tile):
    return jnp.concatenate(
        [tile[r : r + LANES].T for r in range(0, tile.shape[0], LANES)], axis=1
    )


def features(ref, groups, rows=slice(None)):
    mine = lax.axis_index("tgt")
    size = ref.shape[1] // groups
    places = [pl.ds(pl.multiple_of((mine ^ t) * size, LANES), size) for t in range(groups)]
    return jnp.concatenate([ref[rows, place] for place in places], axis=1)


def source_rows(piece, first, count):
    columns = []
    for parts in piece:
        at, found = 0, []
        for part in parts:
            low, high = max(first, at), min(first + count, at + part.shape[0])
            if low < high:
                found.append(part[low - at : high - at, :])
            at += part.shape[0]
        columns.append(jnp.concatenate(found, axis=0))
    return jnp.concatenate(columns, axis=1)


def cosine_block(pieces, targets, inv_src, inv_tgt, cos_ref, rows, cols, work):
    groups = len(pieces[0])
    lhs = jnp.concatenate([features(ref, groups) for ref in targets], axis=0)
    n_tgt = lhs.shape[0]
    step = 2 * LANES
    first = 0
    for piece in pieces:
        n_rows = sum(part.shape[0] for part in piece[0])
        for n in range(0, n_rows, step):
            rhs = source_rows(piece, n, step)
            if inv_src[0] is None:
                inverse = turn(inverse_norms(rhs))[0:SUBLANES]
                inv_src[1][:, n : n + step] = inverse
            work[:, first : first + step] = lax.dot_general(
                lhs, rhs, (((1,), (1,)), ((), ())), preferred_element_type=jnp.float32
            )
            first += step
    if inv_tgt[0] is None:
        inv_tgt[1][...] = inverse_norms(lhs)
    inv_t = inv_tgt[0] if inv_tgt[0] is not None else inv_tgt[1]
    col_lists = [[] for _ in range(0, n_tgt, LANES)]
    first = 0
    for b, piece in enumerate(pieces):
        n_rows = sum(part.shape[0] for part in piece[0])
        inv_s = inv_src[0][b] if inv_src[0] is not None else inv_src[1]
        for n in range(0, n_rows, LANES):
            scale = jnp.broadcast_to(inv_s[0:1, n : n + LANES], (LANES, LANES))
            row_lists = []
            if rows[0] is not None:
                row_lists.append([rows[0][b][k, :, n : n + LANES] for k in range(K)])
            for t in range(0, n_tgt, LANES):
                tile = work[t : t + LANES, first : first + LANES] * scale * inv_t[t : t + LANES]
                cos_ref[t : t + LANES, first : first + LANES] = tile
                row_lists.append(fold(tile))
                col_lists[t // LANES].append(fold(tile.T))
            rows[1](b, n, reduce_lists(row_lists))
            first += LANES
    for line, lists in enumerate(col_lists):
        if cols[0] is not None:
            place = slice(line * LANES, (line + 1) * LANES)
            lists.append([cols[0][k, :, place] for k in range(K)])
        cols[1](line, reduce_lists(lists))


def store_running(ref):
    def store(*at):
        *place, values = at
        first = place[-1] if len(place) > 1 else place[0] * LANES
        for k in range(K):
            ref[k, :, first : first + LANES] = values[k]

    return store


def first_kernel(piece, targets, cos_out, inv_src, inv_tgt, rows, cols, work, cos_ref, sem):
    cosine_block(
        [piece], targets, (None, inv_src), (None, inv_tgt), cos_ref,
        (None, store_running(rows)), (None, store_running(cols)), work,
    )
    pltpu.make_async_copy(cos_ref, cos_out, sem).start()
    pltpu.make_async_copy(cos_ref, cos_out, sem).wait()


def next_kernel(piece, targets, inv_tgt, cols_in, cos_ref, inv_src, rows, cols, work):
    cosine_block(
        [piece], targets, (None, inv_src), (inv_tgt, None), cos_ref,
        (None, store_running(rows)), (cols_in, store_running(cols)), work,
    )


def last_kernel(pieces, targets, inv_src, rows_in, cols_in, cos_ref, row_ref, col_ref, work, inv_tgt):
    lines = cols_in.shape[2] // LANES
    slot = rows_in[0].shape[2] // LANES

    def store_row(b, n, values):
        store_lists(row_ref, fold_sublanes(values), b * slot + n // LANES)

    def store_col(line, values):
        store_lists(col_ref, fold_sublanes(values), lines + line)

    cosine_block(
        pieces, targets, (inv_src, None), (None, inv_tgt), cos_ref,
        (rows_in, store_row), (None, store_col), work,
    )
    for line in range(lines):
        place = slice(line * LANES, (line + 1) * LANES)
        store_lists(col_ref, fold_sublanes([cols_in[k, :, place] for k in range(K)]), line)


def flipped(ref, k, unit):
    if unit >= LANES:
        step = unit // LANES
        firsts = [line ^ step for line in range(0, ref.shape[1], step)]
        return jnp.concatenate([ref[k, first : first + step, :] for first in firsts], axis=0)
    values = ref[k]
    if unit:
        lane = lax.broadcasted_iota(jnp.int32, values.shape, 1)
        up, down = pltpu.roll(values, LANES - unit, 1), pltpu.roll(values, unit, 1)
        values = jnp.where((lane & unit) == 0, up, down)
    return values


def merged(mine, arrived, unit):
    return merge_lists([mine[k] for k in range(K)], [flipped(arrived, k, unit) for k in range(K)])


def merge_kernel(unit, mine, arrived, out_ref):
    for k, values in enumerate(merged(mine, arrived, unit)):
        out_ref[k] = values


def spread(ref, line):
    return jnp.broadcast_to(ref[line : line + 1, :] * 0.5, (LANES, LANES))


def margin_kernel(unit, first, early, late, rows, cols, out_ref, fwd_ref, bwd_ref, bwd_down, held, sem):
    n_early, slot = first.shape
    n_late, n_src = late.shape
    arriving = pltpu.make_async_copy(first, held, sem)
    arriving.start()
    early = [held, *early]
    fwd_ref[...] = sum(merged(*rows, 0)) / K
    bwd_ref[...] = sum(merged(*cols, unit)) / K
    for t in range(0, n_early + n_late, LANES):
        bwd_down[t : t + LANES, :] = spread(bwd_ref, t // LANES).T
    for s in [*range(slot, n_src, LANES), *range(0, slot, LANES)]:
        if s == 0:
            arriving.wait()
        fwd = spread(fwd_ref, s // LANES)
        lists = []
        for t in range(0, n_early + n_late, LANES):
            if t < n_early:
                tile = early[s // slot][t : t + LANES, s % slot : s % slot + LANES]
            else:
                tile = late[t - n_early : t - n_early + LANES, s : s + LANES]
            lists.append(fold(tile / (fwd + bwd_down[t : t + LANES, :])))
        store_lists(out_ref, fold_sublanes(reduce_lists(lists)), s // LANES)


def place_kernel(near, far, lines, known, out_ref):
    at = lax.axis_index("src")
    for b in range(near):
        for a in range(far):
            for c in range(2):
                slot = (b * far + a) * 2 + c
                first = (at ^ ((a * near + b) * 2 + c)) * lines
                out_ref[pl.ds(first, lines), :] = known[slot * lines : (slot + 1) * lines, :]


def prepare_kernel(source, target, source_out, target_out, sems):
    copies = [
        pltpu.make_async_copy(source, source_out, sems.at[0]),
        pltpu.make_async_copy(target, target_out, sems.at[1]),
    ]
    for copy in copies:
        copy.start()
    for copy in copies:
        copy.wait()


def call(kernel, args, out_shapes, scratch=(), flops=0, hbm_in=(), hbm_out=(), sems=0):
    vmem = pl.BlockSpec(memory_space=pltpu.VMEM)
    hbm = pl.BlockSpec(memory_space=pltpu.HBM)
    in_specs = [
        jax.tree.map(lambda _: hbm if n in hbm_in else vmem, arg) for n, arg in enumerate(args)
    ]
    return pl.pallas_call(
        kernel,
        out_shape=tuple(jax.ShapeDtypeStruct(shape, jnp.float32) for shape in out_shapes),
        in_specs=in_specs,
        out_specs=tuple(hbm if n in hbm_out else vmem for n in range(len(out_shapes))),
        scratch_shapes=[pltpu.VMEM(shape, jnp.float32) for shape in scratch]
        + [pltpu.SemaphoreType.DMA] * sems,
        compiler_params=pltpu.CompilerParams(vmem_limit_bytes=16 << 20),
        cost_estimate=pl.CostEstimate(flops=flops, transcendentals=0, bytes_accessed=0),
    )(*args)


def merge_arrays(one, other, unit=0):
    return call(functools.partial(merge_kernel, unit), (one, other), [one.shape])[0]


def prepare(source, target):
    return pl.pallas_call(
        prepare_kernel,
        out_shape=tuple(jax.ShapeDtypeStruct(a.shape, a.dtype) for a in (source, target)),
        in_specs=[pl.BlockSpec(memory_space=pl.ANY)] * 2,
        out_specs=(pl.BlockSpec(memory_space=pltpu.VMEM),) * 2,
        scratch_shapes=[pltpu.SemaphoreType.DMA((2,))],
        compiler_params=pltpu.CompilerParams(vmem_limit_bytes=4 << 20),
        name="prepare",
    )(source, target)


def xor_pairs(size, mask):
    return [(i, i ^ mask) for i in range(size)]


def flip(array, axis, mask):
    shape = array.shape
    split = shape[:axis] + (shape[axis] // (2 * mask), 2, mask) + shape[axis + 1 :]
    parts = array.reshape(split)
    low = lax.slice_in_dim(parts, 0, 1, axis=axis + 1)
    high = lax.slice_in_dim(parts, 1, 2, axis=axis + 1)
    return jnp.concatenate([high, low], axis=axis + 1).reshape(shape)


def flip_where(bit, array, axis, mask):
    return jnp.where(bit != 0, flip(array, axis, mask), array)


def solution(mesh):
    n_src, n_tgt = mesh.shape["src"], mesh.shape["tgt"]
    near = 1 << (((n_src // 2).bit_length() - 1) // 2)
    far = n_src // 2 // near

    def over_src(array, mask):
        return lax.ppermute(array, "src", xor_pairs(n_src, mask))

    def over_tgt(array, mask):
        return lax.ppermute(array, "tgt", xor_pairs(n_tgt, mask))

    def over_both(array, src_mask, tgt_mask):
        pairs = xor_pairs(n_src * n_tgt, src_mask * n_tgt + tgt_mask)
        return lax.ppermute(array, ("src", "tgt"), pairs)

    def local(source, target):
        rows, _ = source.shape
        t_rows, width = target.shape
        own_source, own_target = prepare(source, target)
        pieces = [[None] * n_tgt for _ in range(near)]
        square = (near, n_tgt) == (2, 2)
        held = [own_target] + [None] * (far - 1)
        for t in range(n_tgt):
            for b in range(near):
                if (b, t) == (0, 0):
                    pieces[b][t] = [own_source]
                elif not (square and b and t):
                    pieces[b][t] = [over_both(source, 2 * b, t)]
        for a in range(1, far):
            if (far, a) != (4, 3):
                held[a] = over_src(target, 2 * near * a)
        if square:
            half = rows // 2
            low = over_src(pieces[0][1][0][:half], 2)
            high = over_tgt(pieces[1][0][0][half:], 1)
            pieces[1][1] = [low, high]
        if far == 4:
            held[3] = over_src(held[2], 2 * near)
        pairs = []
        for a in range(far):
            pairs.append([held[a], over_src(held[a] if a else target, 1)])
        n_late = max(1, LANES // (2 * t_rows))
        early = sum(pairs[: far - n_late], [])
        late = sum(pairs[far - n_late :], [])
        e_rows, l_rows = len(early) * t_rows, len(late) * t_rows
        block_src, block_tgt = near * rows, 2 * far * t_rows
        src_lines, tgt_lines = block_src // LANES, block_tgt // LANES
        running = (K, SUBLANES, rows), (K, SUBLANES, e_rows)
        cos, inv, inv_tgt, row_run, cols = call(
            first_kernel, (pieces[0], early),
            [(e_rows, rows), (SUBLANES, rows), (e_rows, LANES), *running],
            [(e_rows, rows)] * 2, 2 * e_rows * rows * width, hbm_out=(0,), sems=1,
        )
        cosines, inverses, row_runs = [cos], [inv], [row_run]
        for b in range(1, near):
            cos, inv, row_run, cols = call(
                next_kernel, (pieces[b], early, inv_tgt, cols),
                [(e_rows, rows), (SUBLANES, rows), *running],
                [(e_rows, rows)], 2 * e_rows * rows * width,
            )
            cosines.append(cos)
            inverses.append(inv)
            row_runs.append(row_run)
        cos_late, row_best, col_best = call(
            last_kernel, (pieces, late, inverses, row_runs, cols),
            [(l_rows, block_src), (K, src_lines, LANES), (K, tgt_lines, LANES)],
            [(l_rows, block_src), (l_rows, LANES)], 2 * l_rows * block_src * width,
        )

        col_best = merge_arrays(col_best, over_src(col_best, 1), t_rows)
        for bit in bits_below(near):
            row_best = merge_arrays(row_best, over_src(row_best, 2 * bit), bit * rows)
        for bit in bits_below(far)[:-1]:
            col_best = merge_arrays(col_best, over_src(col_best, 2 * near * bit), 2 * bit * t_rows)
        for bit in bits_below(n_tgt)[:-1]:
            row_best = merge_arrays(row_best, over_tgt(row_best, bit))
        row_pair = [row_best, over_tgt(row_best, n_tgt // 2)]
        col_pair = [col_best, over_src(col_best, near * far)]
        margins, fwd, bwd = call(
            functools.partial(margin_kernel, far * t_rows),
            (cosines[0], cosines[1:], cos_late, row_pair, col_pair),
            [(K, src_lines, LANES), (src_lines, LANES), (tgt_lines, LANES)],
            [(block_tgt, LANES), cosines[0].shape], hbm_in=(0,), sems=1,
        )
        best = margins.reshape(K, near, rows // LANES, LANES)
        known = bwd.reshape(1, tgt_lines, LANES)
        kept = list(range(near))
        for bit in bits_below(near):
            send = [n for n, slot in enumerate(kept) if slot & bit]
            keep = [n for n, slot in enumerate(kept) if not slot & bit]
            lists = jnp.concatenate([best[:, n : n + 1] for n in send], axis=1)
            split = lists.size // LANES
            payload = jnp.concatenate(
                [lists.reshape(split, LANES), known.reshape(-1, LANES)], axis=0
            )
            arrived = over_src(payload, 2 * bit)
            mine = jnp.concatenate([best[:, n : n + 1] for n in keep], axis=1)
            arrived_lists = arrived[:split].reshape(K, -1, LANES)
            best = merge_arrays(mine.reshape(arrived_lists.shape), arrived_lists).reshape(mine.shape)
            known = jnp.concatenate([known, arrived[split:].reshape(known.shape)], axis=0)
            kept = [kept[n] for n in keep]
        best = best.reshape(K, rows // LANES, LANES)
        for bit in bits_below(n_tgt):
            best = merge_arrays(best, over_tgt(best, bit))
        if t_rows % LANES == 0:
            lines = t_rows // LANES
            (bwd_mean,) = call(
                functools.partial(place_kernel, near, far, lines),
                (known.reshape(-1, LANES),), [(near * tgt_lines, LANES)],
            )
            return fwd[: rows // LANES].reshape(-1), bwd_mean.reshape(-1), best.reshape(K, rows)
        at = lax.axis_index("src")
        known = known.reshape(near, far, 2, t_rows)
        for axis, size, unit in ((0, near, 2), (1, far, 2 * near), (2, 2, 1)):
            for bit in bits_below(size):
                known = flip_where(at & (unit * bit), known, axis, bit)
        bwd_mean = known.transpose(1, 0, 2, 3).reshape(-1)
        return fwd[: rows // LANES].reshape(-1), bwd_mean, best.reshape(K, rows)

    in_specs = (P("src", "tgt"), P(("tgt", "src"), None))
    out_specs = (P("src"), P("tgt"), P(None, "src"))

    return jax.shard_map(local, mesh=mesh, in_specs=in_specs, out_specs=out_specs, check_vma=False)
```

```python
import functools
import math

import jax
import jax.numpy as jnp
from jax import lax
from jax.experimental import pallas as pl
from jax.experimental.pallas import tpu as pltpu
from jax.sharding import PartitionSpec as P

K = 4
LANES = 128
SUBLANES = 8


def bits_below(size):
    return [1 << bit for bit in range(size.bit_length() - 1)]


def exchange(values, upper, lower):
    high = jnp.maximum(values[upper], values[lower])
    values[lower] = jnp.minimum(values[upper], values[lower])
    values[upper] = high


def sort_list(values):
    values = list(values)
    for upper, lower in ((0, 1), (2, 3), (0, 2), (1, 3), (1, 2)):
        exchange(values, upper, lower)
    return values


def merge_lists(one, other):
    values = [jnp.maximum(one[k], other[K - 1 - k]) for k in range(K)]
    for upper, lower in ((0, 2), (1, 3), (0, 1), (2, 3)):
        exchange(values, upper, lower)
    return values


def reduce_lists(lists):
    while len(lists) > 1:
        merged = [merge_lists(lists[n], lists[n + 1]) for n in range(0, len(lists) - 1, 2)]
        lists = merged + lists[len(lists) - len(lists) % 2 :]
    return lists[0]


def fold(tile):
    parts = [tile[r : r + SUBLANES] for r in range(0, tile.shape[0], SUBLANES)]
    return reduce_lists([sort_list(parts[n : n + K]) for n in range(0, len(parts), K)])


def fold_sublanes(values):
    shift = SUBLANES // 2
    while shift:
        values = merge_lists(values, [pltpu.roll(v, shift, 0) for v in values])
        shift //= 2
    return values


def store_lists(ref, values, first):
    for k in range(K):
        for n in range(values[k].shape[1] // LANES):
            ref[k, first + n : first + n + 1, :] = values[k][0:1, n * LANES : (n + 1) * LANES]


def inverse_norms(rows):
    width = rows.shape[1]
    values = rows.astype(jnp.float32)
    total = jnp.sum(values * values, axis=1, keepdims=True)
    inverse = lax.rsqrt(total / width + 1e-06) / math.sqrt(width)
    return jnp.broadcast_to(inverse, (rows.shape[0], LANES))


def turn(tile):
    return jnp.concatenate(
        [tile[r : r + LANES].T for r in range(0, tile.shape[0], LANES)], axis=1
    )


def features(ref, groups, rows=slice(None)):
    mine = lax.axis_index("tgt")
    size = ref.shape[1] // groups
    places = [pl.ds(pl.multiple_of((mine ^ t) * size, LANES), size) for t in range(groups)]
    return jnp.concatenate([ref[rows, place] for place in places], axis=1)


def source_rows(piece, first, count):
    columns = []
    for parts in piece:
        at, found = 0, []
        for part in parts:
            low, high = max(first, at), min(first + count, at + part.shape[0])
            if low < high:
                found.append(part[low - at : high - at, :])
            at += part.shape[0]
        columns.append(jnp.concatenate(found, axis=0))
    return jnp.concatenate(columns, axis=1)


def cosine_block(pieces, targets, inv_src, inv_tgt, cos_ref, rows, cols, work):
    groups = len(pieces[0])
    lhs = jnp.concatenate([features(ref, groups) for ref in targets], axis=0)
    n_tgt = lhs.shape[0]
    step = 2 * LANES
    first = 0
    for piece in pieces:
        n_rows = sum(part.shape[0] for part in piece[0])
        for n in range(0, n_rows, step):
            rhs = source_rows(piece, n, step)
            if inv_src[0] is None:
                inverse = turn(inverse_norms(rhs))[0:SUBLANES]
                inv_src[1][:, n : n + step] = inverse
            work[:, first : first + step] = lax.dot_general(
                lhs, rhs, (((1,), (1,)), ((), ())), preferred_element_type=jnp.float32
            )
            first += step
    if inv_tgt[0] is None:
        inv_tgt[1][...] = inverse_norms(lhs)
    inv_t = inv_tgt[0] if inv_tgt[0] is not None else inv_tgt[1]
    col_lists = [[] for _ in range(0, n_tgt, LANES)]
    first = 0
    for b, piece in enumerate(pieces):
        n_rows = sum(part.shape[0] for part in piece[0])
        inv_s = inv_src[0][b] if inv_src[0] is not None else inv_src[1]
        for n in range(0, n_rows, LANES):
            scale = jnp.broadcast_to(inv_s[0:1, n : n + LANES], (LANES, LANES))
            row_lists = []
            if rows[0] is not None:
                row_lists.append([rows[0][b][k, :, n : n + LANES] for k in range(K)])
            for t in range(0, n_tgt, LANES):
                tile = work[t : t + LANES, first : first + LANES] * scale * inv_t[t : t + LANES]
                cos_ref[t : t + LANES, first : first + LANES] = tile
                row_lists.append(fold(tile))
                col_lists[t // LANES].append(fold(tile.T))
            rows[1](b, n, reduce_lists(row_lists))
            first += LANES
    for line, lists in enumerate(col_lists):
        if cols[0] is not None:
            place = slice(line * LANES, (line + 1) * LANES)
            lists.append([cols[0][k, :, place] for k in range(K)])
        cols[1](line, reduce_lists(lists))


def store_running(ref):
    def store(*at):
        *place, values = at
        first = place[-1] if len(place) > 1 else place[0] * LANES
        for k in range(K):
            ref[k, :, first : first + LANES] = values[k]

    return store


def first_kernel(piece, targets, cos_out, inv_src, inv_tgt, rows, cols, work, cos_ref, sem):
    cosine_block(
        [piece], targets, (None, inv_src), (None, inv_tgt), cos_ref,
        (None, store_running(rows)), (None, store_running(cols)), work,
    )
    pltpu.make_async_copy(cos_ref, cos_out, sem).start()
    pltpu.make_async_copy(cos_ref, cos_out, sem).wait()


def next_kernel(piece, targets, inv_tgt, cols_in, cos_ref, inv_src, rows, cols, work):
    cosine_block(
        [piece], targets, (None, inv_src), (inv_tgt, None), cos_ref,
        (None, store_running(rows)), (cols_in, store_running(cols)), work,
    )


def last_kernel(pieces, targets, inv_src, rows_in, cols_in, cos_ref, row_ref, col_ref, work, inv_tgt):
    lines = cols_in.shape[2] // LANES
    slot = rows_in[0].shape[2] // LANES

    def store_row(b, n, values):
        store_lists(row_ref, fold_sublanes(values), b * slot + n // LANES)

    def store_col(line, values):
        store_lists(col_ref, fold_sublanes(values), lines + line)

    cosine_block(
        pieces, targets, (inv_src, None), (None, inv_tgt), cos_ref,
        (rows_in, store_row), (None, store_col), work,
    )
    for line in range(lines):
        place = slice(line * LANES, (line + 1) * LANES)
        store_lists(col_ref, fold_sublanes([cols_in[k, :, place] for k in range(K)]), line)


def flipped(ref, k, unit):
    step = unit // LANES
    values = ref[k]
    if step:
        lines = [line ^ step for line in range(ref.shape[1])]
        values = jnp.concatenate([ref[k, line : line + 1, :] for line in lines], axis=0)
    lane = lax.broadcasted_iota(jnp.int32, values.shape, 1)
    for bit in bits_below(LANES):
        if unit & bit:
            up, down = pltpu.roll(values, LANES - bit, 1), pltpu.roll(values, bit, 1)
            values = jnp.where((lane & bit) == 0, up, down)
    return values


def merged(mine, arrived, unit):
    return merge_lists([mine[k] for k in range(K)], [flipped(arrived, k, unit) for k in range(K)])


def merge_kernel(unit, mine, arrived, out_ref):
    for k, values in enumerate(merged(mine, arrived, unit)):
        out_ref[k] = values


def spread(ref, line):
    return jnp.broadcast_to(ref[line : line + 1, :] * 0.5, (LANES, LANES))


def margin_kernel(unit, first, early, late, rows, cols, out_ref, fwd_ref, bwd_ref, bwd_down, held, sem):
    n_early, slot = first.shape
    n_late, n_src = late.shape
    arriving = pltpu.make_async_copy(first, held, sem)
    arriving.start()
    early = [held, *early]
    fwd_ref[...] = sum(merged(*rows, 0)) / K
    bwd_ref[...] = sum(merged(*cols, unit)) / K
    for t in range(0, n_early + n_late, LANES):
        bwd_down[t : t + LANES, :] = spread(bwd_ref, t // LANES).T
    for s in [*range(slot, n_src, LANES), *range(0, slot, LANES)]:
        if s == 0:
            arriving.wait()
        fwd = spread(fwd_ref, s // LANES)
        lists = []
        for t in range(0, n_early + n_late, LANES):
            if t < n_early:
                tile = early[s // slot][t : t + LANES, s % slot : s % slot + LANES]
            else:
                tile = late[t - n_early : t - n_early + LANES, s : s + LANES]
            lists.append(fold(tile / (fwd + bwd_down[t : t + LANES, :])))
        store_lists(out_ref, fold_sublanes(reduce_lists(lists)), s // LANES)


def place_kernel(near, far, lines, known, out_ref):
    at = lax.axis_index("src")
    for b in range(near):
        for a in range(far):
            for c in range(2):
                slot = (b * far + a) * 2 + c
                first = (at ^ ((a * near + b) * 2 + c)) * lines
                out_ref[pl.ds(first, lines), :] = known[slot * lines : (slot + 1) * lines, :]


def prepare_kernel(source, target, source_out, target_out, sems):
    copies = [
        pltpu.make_async_copy(source, source_out, sems.at[0]),
        pltpu.make_async_copy(target, target_out, sems.at[1]),
    ]
    for copy in copies:
        copy.start()
    for copy in copies:
        copy.wait()


def call(kernel, args, out_shapes, scratch=(), flops=0, hbm_in=(), hbm_out=(), sems=0):
    vmem = pl.BlockSpec(memory_space=pltpu.VMEM)
    hbm = pl.BlockSpec(memory_space=pltpu.HBM)
    in_specs = [
        jax.tree.map(lambda _: hbm if n in hbm_in else vmem, arg) for n, arg in enumerate(args)
    ]
    return pl.pallas_call(
        kernel,
        out_shape=tuple(jax.ShapeDtypeStruct(shape, jnp.float32) for shape in out_shapes),
        in_specs=in_specs,
        out_specs=tuple(hbm if n in hbm_out else vmem for n in range(len(out_shapes))),
        scratch_shapes=[pltpu.VMEM(shape, jnp.float32) for shape in scratch]
        + [pltpu.SemaphoreType.DMA] * sems,
        compiler_params=pltpu.CompilerParams(vmem_limit_bytes=16 << 20),
        cost_estimate=pl.CostEstimate(flops=flops, transcendentals=0, bytes_accessed=0),
    )(*args)


def merge_arrays(one, other, unit=0):
    return call(functools.partial(merge_kernel, unit), (one, other), [one.shape])[0]


def prepare(source, target):
    return pl.pallas_call(
        prepare_kernel,
        out_shape=tuple(jax.ShapeDtypeStruct(a.shape, a.dtype) for a in (source, target)),
        in_specs=[pl.BlockSpec(memory_space=pl.ANY)] * 2,
        out_specs=(pl.BlockSpec(memory_space=pltpu.VMEM),) * 2,
        scratch_shapes=[pltpu.SemaphoreType.DMA((2,))],
        compiler_params=pltpu.CompilerParams(vmem_limit_bytes=4 << 20),
        name="prepare",
    )(source, target)


def xor_pairs(size, mask):
    return [(i, i ^ mask) for i in range(size)]


def flip(array, axis, mask):
    shape = array.shape
    split = shape[:axis] + (shape[axis] // (2 * mask), 2, mask) + shape[axis + 1 :]
    parts = array.reshape(split)
    low = lax.slice_in_dim(parts, 0, 1, axis=axis + 1)
    high = lax.slice_in_dim(parts, 1, 2, axis=axis + 1)
    return jnp.concatenate([high, low], axis=axis + 1).reshape(shape)


def flip_where(bit, array, axis, mask):
    return jnp.where(bit != 0, flip(array, axis, mask), array)


def solution(mesh):
    n_src, n_tgt = mesh.shape["src"], mesh.shape["tgt"]
    near = 1 << (((n_src // 2).bit_length() - 1) // 2)
    far = n_src // 2 // near

    def over_src(array, mask):
        return lax.ppermute(array, "src", xor_pairs(n_src, mask))

    def over_tgt(array, mask):
        return lax.ppermute(array, "tgt", xor_pairs(n_tgt, mask))

    def over_both(array, src_mask, tgt_mask):
        pairs = xor_pairs(n_src * n_tgt, src_mask * n_tgt + tgt_mask)
        return lax.ppermute(array, ("src", "tgt"), pairs)

    def local(source, target):
        rows, _ = source.shape
        t_rows, width = target.shape
        own_source, own_target = prepare(source, target)
        pieces = [[None] * n_tgt for _ in range(near)]
        square = (near, n_tgt) == (2, 2)
        held = [own_target] + [None] * (far - 1)
        for t in range(n_tgt):
            for b in range(near):
                if (b, t) == (0, 0):
                    pieces[b][t] = [own_source]
                elif not (square and b and t):
                    pieces[b][t] = [over_both(source, 2 * b, t)]
        for a in range(1, far):
            if (far, a) != (4, 3):
                held[a] = over_src(target, 2 * near * a)
        if square:
            half = rows // 2
            low = over_src(pieces[0][1][0][:half], 2)
            high = over_tgt(pieces[1][0][0][half:], 1)
            pieces[1][1] = [low, high]
        if far == 4:
            held[3] = over_src(held[2], 2 * near)
        pairs = []
        for a in range(far):
            pairs.append([held[a], over_src(held[a] if a else target, 1)])
        n_late = max(1, LANES // (2 * t_rows))
        early = sum(pairs[: far - n_late], [])
        late = sum(pairs[far - n_late :], [])
        e_rows, l_rows = len(early) * t_rows, len(late) * t_rows
        block_src, block_tgt = near * rows, 2 * far * t_rows
        src_lines, tgt_lines = block_src // LANES, block_tgt // LANES
        running = (K, SUBLANES, rows), (K, SUBLANES, e_rows)
        cos, inv, inv_tgt, row_run, cols = call(
            first_kernel, (pieces[0], early),
            [(e_rows, rows), (SUBLANES, rows), (e_rows, LANES), *running],
            [(e_rows, rows)] * 2, 2 * e_rows * rows * width, hbm_out=(0,), sems=1,
        )
        cosines, inverses, row_runs = [cos], [inv], [row_run]
        for b in range(1, near):
            cos, inv, row_run, cols = call(
                next_kernel, (pieces[b], early, inv_tgt, cols),
                [(e_rows, rows), (SUBLANES, rows), *running],
                [(e_rows, rows)], 2 * e_rows * rows * width,
            )
            cosines.append(cos)
            inverses.append(inv)
            row_runs.append(row_run)
        cos_late, row_best, col_best = call(
            last_kernel, (pieces, late, inverses, row_runs, cols),
            [(l_rows, block_src), (K, src_lines, LANES), (K, tgt_lines, LANES)],
            [(l_rows, block_src), (l_rows, LANES)], 2 * l_rows * block_src * width,
        )

        col_best = merge_arrays(col_best, over_src(col_best, 1), t_rows)
        for bit in bits_below(near):
            row_best = merge_arrays(row_best, over_src(row_best, 2 * bit), bit * rows)
        for bit in bits_below(far)[:-1]:
            col_best = merge_arrays(col_best, over_src(col_best, 2 * near * bit + 1), (2 * bit + 1) * t_rows)
        for bit in bits_below(n_tgt)[:-1]:
            row_best = merge_arrays(row_best, over_tgt(row_best, bit))
        row_pair = [row_best, over_tgt(row_best, n_tgt // 2)]
        col_pair = [col_best, over_src(col_best, near * far + 1)]
        margins, fwd, bwd = call(
            functools.partial(margin_kernel, (far + 1) * t_rows),
            (cosines[0], cosines[1:], cos_late, row_pair, col_pair),
            [(K, src_lines, LANES), (src_lines, LANES), (tgt_lines, LANES)],
            [(block_tgt, LANES), cosines[0].shape], hbm_in=(0,), sems=1,
        )
        best = margins.reshape(K, near, rows // LANES, LANES)
        known = bwd.reshape(1, tgt_lines, LANES)
        kept = list(range(near))
        for bit in bits_below(near):
            send = [n for n, slot in enumerate(kept) if slot & bit]
            keep = [n for n, slot in enumerate(kept) if not slot & bit]
            lists = jnp.concatenate([best[:, n : n + 1] for n in send], axis=1)
            split = lists.size // LANES
            payload = jnp.concatenate(
                [lists.reshape(split, LANES), known.reshape(-1, LANES)], axis=0
            )
            arrived = over_src(payload, 2 * bit)
            mine = jnp.concatenate([best[:, n : n + 1] for n in keep], axis=1)
            arrived_lists = arrived[:split].reshape(K, -1, LANES)
            best = merge_arrays(mine.reshape(arrived_lists.shape), arrived_lists).reshape(mine.shape)
            known = jnp.concatenate([known, arrived[split:].reshape(known.shape)], axis=0)
            kept = [kept[n] for n in keep]
        best = best.reshape(K, rows // LANES, LANES)
        for bit in bits_below(n_tgt):
            best = merge_arrays(best, over_tgt(best, bit))
        if t_rows % LANES == 0:
            lines = t_rows // LANES
            (bwd_mean,) = call(
                functools.partial(place_kernel, near, far, lines),
                (known.reshape(-1, LANES),), [(near * tgt_lines, LANES)],
            )
            return fwd[: rows // LANES].reshape(-1), bwd_mean.reshape(-1), best.reshape(K, rows)
        at = lax.axis_index("src")
        known = known.reshape(near, far, 2, t_rows)
        for axis, size, unit in ((0, near, 2), (1, far, 2 * near), (2, 2, 1)):
            for bit in bits_below(size):
                known = flip_where(at & (unit * bit), known, axis, bit)
        bwd_mean = known.transpose(1, 0, 2, 3).reshape(-1)
        return fwd[: rows // LANES].reshape(-1), bwd_mean, best.reshape(K, rows)

    in_specs = (P("src", "tgt"), P(("tgt", "src"), None))
    out_specs = (P("src"), P("tgt"), P(None, "src"))

    return jax.shard_map(local, mesh=mesh, in_specs=in_specs, out_specs=out_specs, check_vma=False)
```

```python
import functools
import math

import jax
import jax.numpy as jnp
from jax import lax
from jax.experimental import pallas as pl
from jax.experimental.pallas import tpu as pltpu
from jax.sharding import PartitionSpec as P

K = 4
LANES = 128
SUBLANES = 8


def bits_below(size):
    return [1 << bit for bit in range(size.bit_length() - 1)]


def exchange(values, upper, lower):
    high = jnp.maximum(values[upper], values[lower])
    values[lower] = jnp.minimum(values[upper], values[lower])
    values[upper] = high


def sort_list(values):
    values = list(values)
    for upper, lower in ((0, 1), (2, 3), (0, 2), (1, 3), (1, 2)):
        exchange(values, upper, lower)
    return values


def merge_lists(one, other):
    values = [jnp.maximum(one[k], other[K - 1 - k]) for k in range(K)]
    for upper, lower in ((0, 2), (1, 3), (0, 1), (2, 3)):
        exchange(values, upper, lower)
    return values


def reduce_lists(lists):
    while len(lists) > 1:
        merged = [merge_lists(lists[n], lists[n + 1]) for n in range(0, len(lists) - 1, 2)]
        lists = merged + lists[len(lists) - len(lists) % 2 :]
    return lists[0]


def fold(tile):
    parts = [tile[r : r + SUBLANES] for r in range(0, tile.shape[0], SUBLANES)]
    return reduce_lists([sort_list(parts[n : n + K]) for n in range(0, len(parts), K)])


def fold_sublanes(values):
    shift = SUBLANES // 2
    while shift:
        values = merge_lists(values, [pltpu.roll(v, shift, 0) for v in values])
        shift //= 2
    return values


def store_lists(ref, values, first):
    for k in range(K):
        for n in range(values[k].shape[1] // LANES):
            ref[k, first + n : first + n + 1, :] = values[k][0:1, n * LANES : (n + 1) * LANES]


def inverse_norms(rows):
    width = rows.shape[1]
    values = rows.astype(jnp.float32)
    total = jnp.sum(values * values, axis=1, keepdims=True)
    inverse = lax.rsqrt(total / width + 1e-06) / math.sqrt(width)
    return jnp.broadcast_to(inverse, (rows.shape[0], LANES))


def turn(tile):
    return jnp.concatenate(
        [tile[r : r + LANES].T for r in range(0, tile.shape[0], LANES)], axis=1
    )


def features(ref, groups, rows=slice(None)):
    mine = lax.axis_index("tgt")
    size = ref.shape[1] // groups
    places = [pl.ds(pl.multiple_of((mine ^ t) * size, LANES), size) for t in range(groups)]
    return jnp.concatenate([ref[rows, place] for place in places], axis=1)


def source_rows(piece, first, count):
    columns = []
    for parts in piece:
        at, found = 0, []
        for part in parts:
            low, high = max(first, at), min(first + count, at + part.shape[0])
            if low < high:
                found.append(part[low - at : high - at, :])
            at += part.shape[0]
        columns.append(jnp.concatenate(found, axis=0))
    return jnp.concatenate(columns, axis=1)


def cosine_block(pieces, targets, inv_src, inv_tgt, cos_ref, rows, cols, work):
    groups = len(pieces[0])
    lhs = jnp.concatenate([features(ref, groups) for ref in targets], axis=0)
    n_tgt = lhs.shape[0]
    step = 2 * LANES
    first = 0
    for piece in pieces:
        n_rows = sum(part.shape[0] for part in piece[0])
        for n in range(0, n_rows, step):
            rhs = source_rows(piece, n, step)
            if inv_src[0] is None:
                inverse = turn(inverse_norms(rhs))[0:SUBLANES]
                inv_src[1][:, n : n + step] = inverse
            work[:, first : first + step] = lax.dot_general(
                lhs, rhs, (((1,), (1,)), ((), ())), preferred_element_type=jnp.float32
            )
            first += step
    if inv_tgt[0] is None:
        inv_tgt[1][...] = inverse_norms(lhs)
    inv_t = inv_tgt[0] if inv_tgt[0] is not None else inv_tgt[1]
    col_lists = [[] for _ in range(0, n_tgt, LANES)]
    first = 0
    for b, piece in enumerate(pieces):
        n_rows = sum(part.shape[0] for part in piece[0])
        inv_s = inv_src[0][b] if inv_src[0] is not None else inv_src[1]
        for n in range(0, n_rows, LANES):
            scale = jnp.broadcast_to(inv_s[0:1, n : n + LANES], (LANES, LANES))
            row_lists = []
            if rows[0] is not None:
                row_lists.append([rows[0][b][k, :, n : n + LANES] for k in range(K)])
            for t in range(0, n_tgt, LANES):
                tile = work[t : t + LANES, first : first + LANES] * scale * inv_t[t : t + LANES]
                cos_ref[t : t + LANES, first : first + LANES] = tile
                row_lists.append(fold(tile))
                col_lists[t // LANES].append(fold(tile.T))
            rows[1](b, n, reduce_lists(row_lists))
            first += LANES
    for line, lists in enumerate(col_lists):
        if cols[0] is not None:
            place = slice(line * LANES, (line + 1) * LANES)
            lists.append([cols[0][k, :, place] for k in range(K)])
        cols[1](line, reduce_lists(lists))


def store_running(ref):
    def store(*at):
        *place, values = at
        first = place[-1] if len(place) > 1 else place[0] * LANES
        for k in range(K):
            ref[k, :, first : first + LANES] = values[k]

    return store


def first_kernel(piece, targets, cos_out, inv_src, inv_tgt, rows, cols, work, cos_ref, sem):
    cosine_block(
        [piece], targets, (None, inv_src), (None, inv_tgt), cos_ref,
        (None, store_running(rows)), (None, store_running(cols)), work,
    )
    pltpu.make_async_copy(cos_ref, cos_out, sem).start()
    pltpu.make_async_copy(cos_ref, cos_out, sem).wait()


def next_kernel(piece, targets, inv_tgt, cols_in, cos_ref, inv_src, rows, cols, work):
    cosine_block(
        [piece], targets, (None, inv_src), (inv_tgt, None), cos_ref,
        (None, store_running(rows)), (cols_in, store_running(cols)), work,
    )


def last_kernel(pieces, targets, inv_src, rows_in, cols_in, cos_ref, row_ref, col_ref, work, inv_tgt):
    lines = cols_in.shape[2] // LANES
    slot = rows_in[0].shape[2] // LANES

    def store_row(b, n, values):
        store_lists(row_ref, fold_sublanes(values), b * slot + n // LANES)

    def store_col(line, values):
        store_lists(col_ref, fold_sublanes(values), lines + line)

    cosine_block(
        pieces, targets, (inv_src, None), (None, inv_tgt), cos_ref,
        (rows_in, store_row), (None, store_col), work,
    )
    for line in range(lines):
        place = slice(line * LANES, (line + 1) * LANES)
        store_lists(col_ref, fold_sublanes([cols_in[k, :, place] for k in range(K)]), line)


def flipped(ref, k, unit):
    step = unit // LANES
    values = ref[k]
    if step:
        lines = [line ^ step for line in range(ref.shape[1])]
        values = jnp.concatenate([ref[k, line : line + 1, :] for line in lines], axis=0)
    lane = lax.broadcasted_iota(jnp.int32, values.shape, 1)
    for bit in bits_below(LANES):
        if unit & bit:
            up, down = pltpu.roll(values, LANES - bit, 1), pltpu.roll(values, bit, 1)
            values = jnp.where((lane & bit) == 0, up, down)
    return values


def merged(mine, arrived, unit):
    return merge_lists([mine[k] for k in range(K)], [flipped(arrived, k, unit) for k in range(K)])


def merge_kernel(unit, mine, arrived, out_ref):
    for k, values in enumerate(merged(mine, arrived, unit)):
        out_ref[k] = values


def spread(ref, line):
    return jnp.broadcast_to(ref[line : line + 1, :] * 0.5, (LANES, LANES))


def margin_kernel(unit, first, early, late, rows, cols, out_ref, fwd_ref, bwd_ref, bwd_down, held, sem):
    n_early, slot = first.shape
    n_late, n_src = late.shape
    arriving = pltpu.make_async_copy(first, held, sem)
    arriving.start()
    early = [held, *early]
    fwd_ref[...] = sum(merged(*rows, 0)) / K
    bwd_ref[...] = sum(merged(*cols, unit)) / K
    for t in range(0, n_early + n_late, LANES):
        bwd_down[t : t + LANES, :] = spread(bwd_ref, t // LANES).T
    for s in [*range(slot, n_src, LANES), *range(0, slot, LANES)]:
        if s == 0:
            arriving.wait()
        fwd = spread(fwd_ref, s // LANES)
        lists = []
        for t in range(0, n_early + n_late, LANES):
            if t < n_early:
                tile = early[s // slot][t : t + LANES, s % slot : s % slot + LANES]
            else:
                tile = late[t - n_early : t - n_early + LANES, s : s + LANES]
            lists.append(fold(tile / (fwd + bwd_down[t : t + LANES, :])))
        store_lists(out_ref, fold_sublanes(reduce_lists(lists)), s // LANES)


def place_kernel(near, far, lines, known, out_ref):
    at = lax.axis_index("src")
    for b in range(near):
        for a in range(far):
            for c in range(2):
                slot = (b * far + a) * 2 + c
                first = (at ^ ((a * near + b) * 2 + c)) * lines
                out_ref[pl.ds(first, lines), :] = known[slot * lines : (slot + 1) * lines, :]


def prepare_kernel(source, target, source_out, target_out, sems):
    copies = [
        pltpu.make_async_copy(source, source_out, sems.at[0]),
        pltpu.make_async_copy(target, target_out, sems.at[1]),
    ]
    for copy in copies:
        copy.start()
    for copy in copies:
        copy.wait()


def call(kernel, args, out_shapes, scratch=(), flops=0, hbm_in=(), hbm_out=(), sems=0):
    vmem = pl.BlockSpec(memory_space=pltpu.VMEM)
    hbm = pl.BlockSpec(memory_space=pltpu.HBM)
    in_specs = [
        jax.tree.map(lambda _: hbm if n in hbm_in else vmem, arg) for n, arg in enumerate(args)
    ]
    return pl.pallas_call(
        kernel,
        out_shape=tuple(jax.ShapeDtypeStruct(shape, jnp.float32) for shape in out_shapes),
        in_specs=in_specs,
        out_specs=tuple(hbm if n in hbm_out else vmem for n in range(len(out_shapes))),
        scratch_shapes=[pltpu.VMEM(shape, jnp.float32) for shape in scratch]
        + [pltpu.SemaphoreType.DMA] * sems,
        compiler_params=pltpu.CompilerParams(vmem_limit_bytes=16 << 20),
        cost_estimate=pl.CostEstimate(flops=flops, transcendentals=0, bytes_accessed=0),
    )(*args)


def merge_arrays(one, other, unit=0):
    return call(functools.partial(merge_kernel, unit), (one, other), [one.shape])[0]


def prepare(source, target):
    return pl.pallas_call(
        prepare_kernel,
        out_shape=tuple(jax.ShapeDtypeStruct(a.shape, a.dtype) for a in (source, target)),
        in_specs=[pl.BlockSpec(memory_space=pl.ANY)] * 2,
        out_specs=(pl.BlockSpec(memory_space=pltpu.VMEM),) * 2,
        scratch_shapes=[pltpu.SemaphoreType.DMA((2,))],
        compiler_params=pltpu.CompilerParams(vmem_limit_bytes=4 << 20),
        name="prepare",
    )(source, target)


def xor_pairs(size, mask):
    return [(i, i ^ mask) for i in range(size)]


def flip(array, axis, mask):
    shape = array.shape
    split = shape[:axis] + (shape[axis] // (2 * mask), 2, mask) + shape[axis + 1 :]
    parts = array.reshape(split)
    low = lax.slice_in_dim(parts, 0, 1, axis=axis + 1)
    high = lax.slice_in_dim(parts, 1, 2, axis=axis + 1)
    return jnp.concatenate([high, low], axis=axis + 1).reshape(shape)


def flip_where(bit, array, axis, mask):
    return jnp.where(bit != 0, flip(array, axis, mask), array)


def solution(mesh):
    n_src, n_tgt = mesh.shape["src"], mesh.shape["tgt"]
    near = 1 << (((n_src // 2).bit_length() - 1) // 2)
    far = n_src // 2 // near

    def over_src(array, mask):
        return lax.ppermute(array, "src", xor_pairs(n_src, mask))

    def over_tgt(array, mask):
        return lax.ppermute(array, "tgt", xor_pairs(n_tgt, mask))

    def over_both(array, src_mask, tgt_mask):
        pairs = xor_pairs(n_src * n_tgt, src_mask * n_tgt + tgt_mask)
        return lax.ppermute(array, ("src", "tgt"), pairs)

    def local(source, target):
        rows, _ = source.shape
        t_rows, width = target.shape
        own_source, own_target = prepare(source, target)
        pieces = [[None] * n_tgt for _ in range(near)]
        square = (near, n_tgt) == (2, 2)
        held = [own_target] + [None] * (far - 1)
        for t in range(n_tgt):
            for b in range(near):
                if (b, t) == (0, 0):
                    pieces[b][t] = [own_source]
                elif not (square and b and t):
                    pieces[b][t] = [over_both(source, 2 * b, t)]
        for a in range(1, far):
            if (far, a) != (4, 3):
                held[a] = over_src(target, 2 * near * a)
        if square:
            half = rows // 2
            low = over_src(pieces[0][1][0][:half], 2)
            high = over_tgt(pieces[1][0][0][half:], 1)
            pieces[1][1] = [low, high]
        if far == 4:
            held[3] = over_src(held[2], 2 * near)
        pairs = []
        for a in range(far):
            pairs.append([held[a], over_src(held[a] if a else target, 1)])
        n_late = max(1, LANES // (2 * t_rows))
        early = sum(pairs[: far - n_late], [])
        late = sum(pairs[far - n_late :], [])
        e_rows, l_rows = len(early) * t_rows, len(late) * t_rows
        block_src, block_tgt = near * rows, 2 * far * t_rows
        src_lines, tgt_lines = block_src // LANES, block_tgt // LANES
        running = (K, SUBLANES, rows), (K, SUBLANES, e_rows)
        cos, inv, inv_tgt, row_run, cols = call(
            first_kernel, (pieces[0], early),
            [(e_rows, rows), (SUBLANES, rows), (e_rows, LANES), *running],
            [(e_rows, rows)] * 2, 2 * e_rows * rows * width, hbm_out=(0,), sems=1,
        )
        cosines, inverses, row_runs = [cos], [inv], [row_run]
        for b in range(1, near):
            cos, inv, row_run, cols = call(
                next_kernel, (pieces[b], early, inv_tgt, cols),
                [(e_rows, rows), (SUBLANES, rows), *running],
                [(e_rows, rows)], 2 * e_rows * rows * width,
            )
            cosines.append(cos)
            inverses.append(inv)
            row_runs.append(row_run)
        cos_late, row_best, col_best = call(
            last_kernel, (pieces, late, inverses, row_runs, cols),
            [(l_rows, block_src), (K, src_lines, LANES), (K, tgt_lines, LANES)],
            [(l_rows, block_src), (l_rows, LANES)], 2 * l_rows * block_src * width,
        )

        arrived = over_src(col_best, 1)
        col_best = merge_arrays(col_best, arrived, t_rows)
        for bit in bits_below(near):
            arrived = over_src(row_best, 2 * bit)
            row_best = merge_arrays(row_best, arrived, bit * rows)
        for bit in bits_below(n_tgt):
            arrived = over_tgt(row_best, bit)
            if 2 * bit < n_tgt:
                row_best = merge_arrays(row_best, arrived)
        row_pair = [row_best, arrived]
        for bit in bits_below(far):
            arrived = over_src(col_best, 2 * near * bit + 1)
            if 2 * bit < far:
                col_best = merge_arrays(col_best, arrived, (2 * bit + 1) * t_rows)
        col_pair = [col_best, arrived]
        margins, fwd, bwd = call(
            functools.partial(margin_kernel, (far + 1) * t_rows),
            (cosines[0], cosines[1:], cos_late, row_pair, col_pair),
            [(K, src_lines, LANES), (src_lines, LANES), (tgt_lines, LANES)],
            [(block_tgt, LANES), cosines[0].shape], hbm_in=(0,), sems=1,
        )
        best = margins.reshape(K, near, rows // LANES, LANES)
        known = bwd.reshape(1, tgt_lines, LANES)
        kept = list(range(near))
        for bit in bits_below(near):
            send = [n for n, slot in enumerate(kept) if slot & bit]
            keep = [n for n, slot in enumerate(kept) if not slot & bit]
            lists = jnp.concatenate([best[:, n : n + 1] for n in send], axis=1)
            split = lists.size // LANES
            payload = jnp.concatenate(
                [lists.reshape(split, LANES), known.reshape(-1, LANES)], axis=0
            )
            arrived = over_src(payload, 2 * bit)
            mine = jnp.concatenate([best[:, n : n + 1] for n in keep], axis=1)
            arrived_lists = arrived[:split].reshape(K, -1, LANES)
            best = merge_arrays(mine.reshape(arrived_lists.shape), arrived_lists).reshape(mine.shape)
            known = jnp.concatenate([known, arrived[split:].reshape(known.shape)], axis=0)
            kept = [kept[n] for n in keep]
        best = best.reshape(K, rows // LANES, LANES)
        for bit in bits_below(n_tgt):
            best = merge_arrays(best, over_tgt(best, bit))
        if t_rows % LANES == 0:
            lines = t_rows // LANES
            (bwd_mean,) = call(
                functools.partial(place_kernel, near, far, lines),
                (known.reshape(-1, LANES),), [(near * tgt_lines, LANES)],
            )
            return fwd[: rows // LANES].reshape(-1), bwd_mean.reshape(-1), best.reshape(K, rows)
        at = lax.axis_index("src")
        known = known.reshape(near, far, 2, t_rows)
        for axis, size, unit in ((0, near, 2), (1, far, 2 * near), (2, 2, 1)):
            for bit in bits_below(size):
                known = flip_where(at & (unit * bit), known, axis, bit)
        bwd_mean = known.transpose(1, 0, 2, 3).reshape(-1)
        return fwd[: rows // LANES].reshape(-1), bwd_mean, best.reshape(K, rows)

    in_specs = (P("src", "tgt"), P(("tgt", "src"), None))
    out_specs = (P("src"), P("tgt"), P(None, "src"))

    return jax.shard_map(local, mesh=mesh, in_specs=in_specs, out_specs=out_specs, check_vma=False)
```

```python
import functools
import math

import jax
import jax.numpy as jnp
from jax import lax
from jax.experimental import pallas as pl
from jax.experimental.pallas import tpu as pltpu
from jax.sharding import PartitionSpec as P

K = 4
LANES = 128
SUBLANES = 8


def bits_below(size):
    return [1 << bit for bit in range(size.bit_length() - 1)]


def exchange(values, upper, lower):
    high = jnp.maximum(values[upper], values[lower])
    values[lower] = jnp.minimum(values[upper], values[lower])
    values[upper] = high


def sort_list(values):
    values = list(values)
    for upper, lower in ((0, 1), (2, 3), (0, 2), (1, 3), (1, 2)):
        exchange(values, upper, lower)
    return values


def merge_lists(one, other):
    values = [jnp.maximum(one[k], other[K - 1 - k]) for k in range(K)]
    for upper, lower in ((0, 2), (1, 3), (0, 1), (2, 3)):
        exchange(values, upper, lower)
    return values


def reduce_lists(lists):
    while len(lists) > 1:
        merged = [merge_lists(lists[n], lists[n + 1]) for n in range(0, len(lists) - 1, 2)]
        lists = merged + lists[len(lists) - len(lists) % 2 :]
    return lists[0]


def fold(tile):
    parts = [tile[r : r + SUBLANES] for r in range(0, tile.shape[0], SUBLANES)]
    return reduce_lists([sort_list(parts[n : n + K]) for n in range(0, len(parts), K)])


def fold_sublanes(values):
    shift = SUBLANES // 2
    while shift:
        values = merge_lists(values, [pltpu.roll(v, shift, 0) for v in values])
        shift //= 2
    return values


def store_lists(ref, values, first):
    for k in range(K):
        for n in range(values[k].shape[1] // LANES):
            ref[k, first + n : first + n + 1, :] = values[k][0:1, n * LANES : (n + 1) * LANES]


def inverse_norms(rows):
    width = rows.shape[1]
    values = rows.astype(jnp.float32)
    total = jnp.sum(values * values, axis=1, keepdims=True)
    inverse = lax.rsqrt(total / width + 1e-06) / math.sqrt(width)
    return jnp.broadcast_to(inverse, (rows.shape[0], LANES))


def turn(tile):
    return jnp.concatenate(
        [tile[r : r + LANES].T for r in range(0, tile.shape[0], LANES)], axis=1
    )


def features(ref, groups, rows=slice(None)):
    mine = lax.axis_index("tgt")
    size = ref.shape[1] // groups
    places = [pl.ds(pl.multiple_of((mine ^ t) * size, LANES), size) for t in range(groups)]
    return jnp.concatenate([ref[rows, place] for place in places], axis=1)


def source_rows(piece, first, count):
    columns = []
    for parts in piece:
        at, found = 0, []
        for part in parts:
            low, high = max(first, at), min(first + count, at + part.shape[0])
            if low < high:
                found.append(part[low - at : high - at, :])
            at += part.shape[0]
        columns.append(jnp.concatenate(found, axis=0))
    return jnp.concatenate(columns, axis=1)


def cosine_block(pieces, targets, inv_src, inv_tgt, cos_ref, rows, cols, work):
    groups = len(pieces[0])
    lhs = jnp.concatenate([features(ref, groups) for ref in targets], axis=0)
    n_tgt = lhs.shape[0]
    step = 2 * LANES
    first = 0
    for piece in pieces:
        n_rows = sum(part.shape[0] for part in piece[0])
        for n in range(0, n_rows, step):
            rhs = source_rows(piece, n, step)
            if inv_src[0] is None:
                inverse = turn(inverse_norms(rhs))[0:SUBLANES]
                inv_src[1][:, n : n + step] = inverse
            work[:, first : first + step] = lax.dot_general(
                lhs, rhs, (((1,), (1,)), ((), ())), preferred_element_type=jnp.float32
            )
            first += step
    if inv_tgt[0] is None:
        inv_tgt[1][...] = inverse_norms(lhs)
    inv_t = inv_tgt[0] if inv_tgt[0] is not None else inv_tgt[1]
    col_lists = [[] for _ in range(0, n_tgt, LANES)]
    first = 0
    for b, piece in enumerate(pieces):
        n_rows = sum(part.shape[0] for part in piece[0])
        inv_s = inv_src[0][b] if inv_src[0] is not None else inv_src[1]
        for n in range(0, n_rows, LANES):
            scale = jnp.broadcast_to(inv_s[0:1, n : n + LANES], (LANES, LANES))
            row_lists = []
            if rows[0] is not None:
                row_lists.append([rows[0][b][k, :, n : n + LANES] for k in range(K)])
            for t in range(0, n_tgt, LANES):
                tile = work[t : t + LANES, first : first + LANES] * scale * inv_t[t : t + LANES]
                cos_ref[t : t + LANES, first : first + LANES] = tile
                row_lists.append(fold(tile))
                col_lists[t // LANES].append(fold(tile.T))
            rows[1](b, n, reduce_lists(row_lists))
            first += LANES
    for line, lists in enumerate(col_lists):
        if cols[0] is not None:
            place = slice(line * LANES, (line + 1) * LANES)
            lists.append([cols[0][k, :, place] for k in range(K)])
        cols[1](line, reduce_lists(lists))


def store_running(ref):
    def store(*at):
        *place, values = at
        first = place[-1] if len(place) > 1 else place[0] * LANES
        for k in range(K):
            ref[k, :, first : first + LANES] = values[k]

    return store


def first_kernel(piece, targets, cos_out, inv_src, inv_tgt, rows, cols, work, cos_ref, sem):
    cosine_block(
        [piece], targets, (None, inv_src), (None, inv_tgt), cos_ref,
        (None, store_running(rows)), (None, store_running(cols)), work,
    )
    pltpu.make_async_copy(cos_ref, cos_out, sem).start()
    pltpu.make_async_copy(cos_ref, cos_out, sem).wait()


def next_kernel(piece, targets, inv_tgt, cols_in, cos_ref, inv_src, rows, cols, work):
    cosine_block(
        [piece], targets, (None, inv_src), (inv_tgt, None), cos_ref,
        (None, store_running(rows)), (cols_in, store_running(cols)), work,
    )


def last_kernel(pieces, targets, inv_src, rows_in, cols_in, cos_ref, row_ref, col_ref, work, inv_tgt):
    lines = cols_in.shape[2] // LANES
    slot = rows_in[0].shape[2] // LANES

    def store_row(b, n, values):
        store_lists(row_ref, fold_sublanes(values), b * slot + n // LANES)

    def store_col(line, values):
        store_lists(col_ref, fold_sublanes(values), lines + line)

    cosine_block(
        pieces, targets, (inv_src, None), (None, inv_tgt), cos_ref,
        (rows_in, store_row), (None, store_col), work,
    )
    for line in range(lines):
        place = slice(line * LANES, (line + 1) * LANES)
        store_lists(col_ref, fold_sublanes([cols_in[k, :, place] for k in range(K)]), line)


def flipped(ref, k, unit):
    step = unit // LANES
    values = ref[k]
    if step:
        lines = [line ^ step for line in range(ref.shape[1])]
        values = jnp.concatenate([ref[k, line : line + 1, :] for line in lines], axis=0)
    lane = lax.broadcasted_iota(jnp.int32, values.shape, 1)
    for bit in bits_below(LANES):
        if unit & bit:
            up, down = pltpu.roll(values, LANES - bit, 1), pltpu.roll(values, bit, 1)
            values = jnp.where((lane & bit) == 0, up, down)
    return values


def merged(mine, arrived, unit):
    return merge_lists([mine[k] for k in range(K)], [flipped(arrived, k, unit) for k in range(K)])


def merge_kernel(unit, mine, arrived, out_ref):
    for k, values in enumerate(merged(mine, arrived, unit)):
        out_ref[k] = values


def output_kernel(mine, arrived, out_ref, held, sem):
    for k, values in enumerate(merged(mine, arrived, 0)):
        for line in range(values.shape[0]):
            held[k : k + 1, line * LANES : (line + 1) * LANES] = values[line : line + 1, :]
    leaving = pltpu.make_async_copy(held, out_ref, sem)
    leaving.start()
    leaving.wait()


def spread(ref, line):
    return jnp.broadcast_to(ref[line : line + 1, :] * 0.5, (LANES, LANES))


def margin_lists(early, late, first, fwd_ref, bwd_down, out_ref):
    n_early, n_late = early.shape[0], late.shape[0]
    for s in range(0, early.shape[1], LANES):
        fwd = spread(fwd_ref, (first + s) // LANES)
        lists = []
        for t in range(0, n_early + n_late, LANES):
            if t < n_early:
                tile = early[t : t + LANES, s : s + LANES]
            else:
                tile = late[t - n_early : t - n_early + LANES, first + s : first + s + LANES]
            lists.append(fold(tile / (fwd + bwd_down[t : t + LANES, :])))
        store_lists(out_ref, fold_sublanes(reduce_lists(lists)), s // LANES)


def sent_kernel(unit, early, late, rows, cols, *outs):
    *lists, fwd_ref, bwd_ref, bwd_down = outs
    fwd_ref[...] = sum(merged(*rows, 0)) / K
    bwd_ref[...] = sum(merged(*cols, unit)) / K
    for line in range(bwd_ref.shape[0]):
        bwd_down[line * LANES : (line + 1) * LANES, :] = spread(bwd_ref, line).T
    for n, out_ref in enumerate(lists):
        margin_lists(early[n], late, (n + 1) * early[n].shape[1], fwd_ref, bwd_down, out_ref)


def kept_kernel(first, late, fwd_ref, bwd_down, out_ref, held, sem):
    arriving = pltpu.make_async_copy(first, held, sem)
    arriving.start()
    arriving.wait()
    margin_lists(held, late, 0, fwd_ref, bwd_down, out_ref)


def place_kernel(near, far, lines, known, out_ref):
    at = lax.axis_index("src")
    for b in range(near):
        for a in range(far):
            for c in range(2):
                slot = (b * far + a) * 2 + c
                first = (at ^ ((a * near + b) * 2 + c)) * lines
                out_ref[pl.ds(first, lines), :] = known[slot * lines : (slot + 1) * lines, :]


def prepare_kernel(source, target, source_out, target_out, sems):
    copies = [
        pltpu.make_async_copy(source, source_out, sems.at[0]),
        pltpu.make_async_copy(target, target_out, sems.at[1]),
    ]
    for copy in copies:
        copy.start()
    for copy in copies:
        copy.wait()


def call(kernel, args, out_shapes, scratch=(), flops=0, hbm_in=(), hbm_out=(), sems=0):
    vmem = pl.BlockSpec(memory_space=pltpu.VMEM)
    hbm = pl.BlockSpec(memory_space=pltpu.HBM)
    in_specs = [
        jax.tree.map(lambda _: hbm if n in hbm_in else vmem, arg) for n, arg in enumerate(args)
    ]
    return pl.pallas_call(
        kernel,
        out_shape=tuple(jax.ShapeDtypeStruct(shape, jnp.float32) for shape in out_shapes),
        in_specs=in_specs,
        out_specs=tuple(hbm if n in hbm_out else vmem for n in range(len(out_shapes))),
        scratch_shapes=[pltpu.VMEM(shape, jnp.float32) for shape in scratch]
        + [pltpu.SemaphoreType.DMA] * sems,
        compiler_params=pltpu.CompilerParams(vmem_limit_bytes=16 << 20),
        cost_estimate=pl.CostEstimate(flops=flops, transcendentals=0, bytes_accessed=0),
    )(*args)


def merge_arrays(one, other, unit=0):
    return call(functools.partial(merge_kernel, unit), (one, other), [one.shape])[0]


def prepare(source, target):
    return pl.pallas_call(
        prepare_kernel,
        out_shape=tuple(jax.ShapeDtypeStruct(a.shape, a.dtype) for a in (source, target)),
        in_specs=[pl.BlockSpec(memory_space=pl.ANY)] * 2,
        out_specs=(pl.BlockSpec(memory_space=pltpu.VMEM),) * 2,
        scratch_shapes=[pltpu.SemaphoreType.DMA((2,))],
        compiler_params=pltpu.CompilerParams(vmem_limit_bytes=4 << 20),
        name="prepare",
    )(source, target)


def xor_pairs(size, mask):
    return [(i, i ^ mask) for i in range(size)]


def flip(array, axis, mask):
    shape = array.shape
    split = shape[:axis] + (shape[axis] // (2 * mask), 2, mask) + shape[axis + 1 :]
    parts = array.reshape(split)
    low = lax.slice_in_dim(parts, 0, 1, axis=axis + 1)
    high = lax.slice_in_dim(parts, 1, 2, axis=axis + 1)
    return jnp.concatenate([high, low], axis=axis + 1).reshape(shape)


def flip_where(bit, array, axis, mask):
    return jnp.where(bit != 0, flip(array, axis, mask), array)


def solution(mesh):
    n_src, n_tgt = mesh.shape["src"], mesh.shape["tgt"]
    near = 1 << (((n_src // 2).bit_length() - 1) // 2)
    far = n_src // 2 // near

    def over_src(array, mask):
        return lax.ppermute(array, "src", xor_pairs(n_src, mask))

    def over_tgt(array, mask):
        return lax.ppermute(array, "tgt", xor_pairs(n_tgt, mask))

    def over_both(array, src_mask, tgt_mask):
        pairs = xor_pairs(n_src * n_tgt, src_mask * n_tgt + tgt_mask)
        return lax.ppermute(array, ("src", "tgt"), pairs)

    def local(source, target):
        rows, _ = source.shape
        t_rows, width = target.shape
        own_source, own_target = prepare(source, target)
        pieces = [[None] * n_tgt for _ in range(near)]
        square = (near, n_tgt) == (2, 2)
        held = [own_target] + [None] * (far - 1)
        for t in range(n_tgt):
            for b in range(near):
                if (b, t) == (0, 0):
                    pieces[b][t] = [own_source]
                elif not (square and b and t):
                    pieces[b][t] = [over_both(source, 2 * b, t)]
        for a in range(1, far):
            if (far, a) != (4, 3):
                held[a] = over_src(target, 2 * near * a)
        if square:
            half = rows // 2
            low = over_src(pieces[0][1][0][:half], 2)
            high = over_tgt(pieces[1][0][0][half:], 1)
            pieces[1][1] = [low, high]
        if far == 4:
            held[3] = over_src(held[2], 2 * near)
        pairs = []
        for a in range(far):
            pairs.append([held[a], over_src(held[a] if a else target, 1)])
        n_late = max(1, LANES // (2 * t_rows))
        early = sum(pairs[: far - n_late], [])
        late = sum(pairs[far - n_late :], [])
        e_rows, l_rows = len(early) * t_rows, len(late) * t_rows
        block_src, block_tgt = near * rows, 2 * far * t_rows
        src_lines, tgt_lines = block_src // LANES, block_tgt // LANES
        running = (K, SUBLANES, rows), (K, SUBLANES, e_rows)
        cos, inv, inv_tgt, row_run, cols = call(
            first_kernel, (pieces[0], early),
            [(e_rows, rows), (SUBLANES, rows), (e_rows, LANES), *running],
            [(e_rows, rows)] * 2, 2 * e_rows * rows * width, hbm_out=(0,), sems=1,
        )
        cosines, inverses, row_runs = [cos], [inv], [row_run]
        for b in range(1, near):
            cos, inv, row_run, cols = call(
                next_kernel, (pieces[b], early, inv_tgt, cols),
                [(e_rows, rows), (SUBLANES, rows), *running],
                [(e_rows, rows)], 2 * e_rows * rows * width,
            )
            cosines.append(cos)
            inverses.append(inv)
            row_runs.append(row_run)
        cos_late, row_best, col_best = call(
            last_kernel, (pieces, late, inverses, row_runs, cols),
            [(l_rows, block_src), (K, src_lines, LANES), (K, tgt_lines, LANES)],
            [(l_rows, block_src), (l_rows, LANES)], 2 * l_rows * block_src * width,
        )

        arrived = over_src(col_best, 1)
        col_best = merge_arrays(col_best, arrived, t_rows)
        for bit in bits_below(near):
            arrived = over_src(row_best, 2 * bit)
            row_best = merge_arrays(row_best, arrived, bit * rows)
        for bit in bits_below(n_tgt):
            arrived = over_tgt(row_best, bit)
            if 2 * bit < n_tgt:
                row_best = merge_arrays(row_best, arrived)
        row_pair = [row_best, arrived]
        for bit in bits_below(far):
            arrived = over_src(col_best, 2 * near * bit + 1)
            if 2 * bit < far:
                col_best = merge_arrays(col_best, arrived, (2 * bit + 1) * t_rows)
        col_pair = [col_best, arrived]
        lines = rows // LANES
        *sent, fwd, bwd, bwd_down = call(
            functools.partial(sent_kernel, (far + 1) * t_rows),
            (cosines[1:], cos_late, row_pair, col_pair),
            [(K, lines, LANES)] * (near - 1)
            + [(src_lines, LANES), (tgt_lines, LANES), (block_tgt, LANES)],
        )
        (own,) = call(
            kept_kernel, (cosines[0], cos_late, fwd, bwd_down),
            [(K, lines, LANES)], [cosines[0].shape], 2 * block_tgt * rows * K, hbm_in=(0,), sems=1,
        )
        best = dict(enumerate([own, *sent]))
        known = bwd.reshape(1, tgt_lines, LANES)
        for bit in bits_below(near):
            send = [slot for slot in best if slot & bit]
            keep = [slot for slot in best if not slot & bit]
            lists = jnp.concatenate([best[slot] for slot in send], axis=1)
            split = lists.size // LANES
            payload = jnp.concatenate(
                [lists.reshape(split, LANES), known.reshape(-1, LANES)], axis=0
            )
            arrived = over_src(payload, 2 * bit)
            mine = jnp.concatenate([best[slot] for slot in keep], axis=1)
            mine = merge_arrays(mine, arrived[:split].reshape(mine.shape))
            best = {slot: mine[:, n * lines : (n + 1) * lines] for n, slot in enumerate(keep)}
            known = jnp.concatenate([known, arrived[split:].reshape(known.shape)], axis=0)
        best = best[0]
        for bit in bits_below(n_tgt)[:-1]:
            best = merge_arrays(best, over_tgt(best, bit))
        (best,) = call(
            output_kernel, (best, over_tgt(best, n_tgt // 2)),
            [(K, rows)], [(K, rows)], hbm_out=(0,), sems=1,
        )
        if t_rows % LANES == 0:
            (bwd_mean,) = call(
                functools.partial(place_kernel, near, far, t_rows // LANES),
                (known.reshape(-1, LANES),), [(near * tgt_lines, LANES)],
            )
            return fwd[: rows // LANES].reshape(-1), bwd_mean.reshape(-1), best
        at = lax.axis_index("src")
        known = known.reshape(near, far, 2, t_rows)
        for axis, size, unit in ((0, near, 2), (1, far, 2 * near), (2, 2, 1)):
            for bit in bits_below(size):
                known = flip_where(at & (unit * bit), known, axis, bit)
        bwd_mean = known.transpose(1, 0, 2, 3).reshape(-1)
        return fwd[: rows // LANES].reshape(-1), bwd_mean, best

    in_specs = (P("src", "tgt"), P(("tgt", "src"), None))
    out_specs = (P("src"), P("tgt"), P(None, "src"))

    return jax.shard_map(local, mesh=mesh, in_specs=in_specs, out_specs=out_specs, check_vma=False)
```

```python
import functools
import math

import jax
import jax.numpy as jnp
from jax import lax
from jax.experimental import pallas as pl
from jax.experimental.pallas import tpu as pltpu
from jax.sharding import PartitionSpec as P

K = 4
LANES = 128
SUBLANES = 8


def bits_below(size):
    return [1 << bit for bit in range(size.bit_length() - 1)]


def exchange(values, upper, lower):
    high = jnp.maximum(values[upper], values[lower])
    values[lower] = jnp.minimum(values[upper], values[lower])
    values[upper] = high


def sort_list(values):
    values = list(values)
    for upper, lower in ((0, 1), (2, 3), (0, 2), (1, 3), (1, 2)):
        exchange(values, upper, lower)
    return values


def merge_lists(one, other):
    values = [jnp.maximum(one[k], other[K - 1 - k]) for k in range(K)]
    for upper, lower in ((0, 2), (1, 3), (0, 1), (2, 3)):
        exchange(values, upper, lower)
    return values


def reduce_lists(lists):
    while len(lists) > 1:
        merged = [merge_lists(lists[n], lists[n + 1]) for n in range(0, len(lists) - 1, 2)]
        lists = merged + lists[len(lists) - len(lists) % 2 :]
    return lists[0]


def fold(tile):
    parts = [tile[r : r + SUBLANES] for r in range(0, tile.shape[0], SUBLANES)]
    return reduce_lists([sort_list(parts[n : n + K]) for n in range(0, len(parts), K)])


def fold_sublanes(values):
    shift = SUBLANES // 2
    while shift:
        values = merge_lists(values, [pltpu.roll(v, shift, 0) for v in values])
        shift //= 2
    return values


def store_lists(ref, values, first):
    for k in range(K):
        for n in range(values[k].shape[1] // LANES):
            ref[k, first + n : first + n + 1, :] = values[k][0:1, n * LANES : (n + 1) * LANES]


def inverse_norms(rows):
    width = rows.shape[1]
    values = rows.astype(jnp.float32)
    total = jnp.sum(values * values, axis=1, keepdims=True)
    inverse = lax.rsqrt(total / width + 1e-06) / math.sqrt(width)
    return jnp.broadcast_to(inverse, (rows.shape[0], LANES))


def turn(tile):
    return jnp.concatenate(
        [tile[r : r + LANES].T for r in range(0, tile.shape[0], LANES)], axis=1
    )


def features(ref, groups, rows=slice(None)):
    mine = lax.axis_index("tgt")
    size = ref.shape[1] // groups
    places = [pl.ds(pl.multiple_of((mine ^ t) * size, LANES), size) for t in range(groups)]
    return jnp.concatenate([ref[rows, place] for place in places], axis=1)


def source_rows(piece, first, count):
    columns = []
    for parts in piece:
        at, found = 0, []
        for part in parts:
            low, high = max(first, at), min(first + count, at + part.shape[0])
            if low < high:
                found.append(part[low - at : high - at, :])
            at += part.shape[0]
        columns.append(jnp.concatenate(found, axis=0))
    return jnp.concatenate(columns, axis=1)


def cosine_block(pieces, targets, inv_src, inv_tgt, cos_ref, rows, cols, work):
    groups = len(pieces[0])
    lhs = jnp.concatenate([features(ref, groups) for ref in targets], axis=0)
    n_tgt = lhs.shape[0]
    step = 2 * LANES
    first = 0
    for piece in pieces:
        n_rows = sum(part.shape[0] for part in piece[0])
        for n in range(0, n_rows, step):
            rhs = source_rows(piece, n, step)
            if inv_src[0] is None:
                inverse = turn(inverse_norms(rhs))[0:SUBLANES]
                inv_src[1][:, n : n + step] = inverse
            work[:, first : first + step] = lax.dot_general(
                lhs, rhs, (((1,), (1,)), ((), ())), preferred_element_type=jnp.float32
            )
            first += step
    if inv_tgt[0] is None:
        inv_tgt[1][...] = inverse_norms(lhs)
    inv_t = inv_tgt[0] if inv_tgt[0] is not None else inv_tgt[1]
    col_lists = [[] for _ in range(0, n_tgt, LANES)]
    first = 0
    for b, piece in enumerate(pieces):
        n_rows = sum(part.shape[0] for part in piece[0])
        inv_s = inv_src[0][b] if inv_src[0] is not None else inv_src[1]
        for n in range(0, n_rows, LANES):
            scale = jnp.broadcast_to(inv_s[0:1, n : n + LANES], (LANES, LANES))
            row_lists = []
            if rows[0] is not None:
                row_lists.append([rows[0][b][k, :, n : n + LANES] for k in range(K)])
            for t in range(0, n_tgt, LANES):
                tile = work[t : t + LANES, first : first + LANES] * scale * inv_t[t : t + LANES]
                cos_ref[t : t + LANES, first : first + LANES] = tile
                row_lists.append(fold(tile))
                col_lists[t // LANES].append(fold(tile.T))
            rows[1](b, n, reduce_lists(row_lists))
            first += LANES
    for line, lists in enumerate(col_lists):
        if cols[0] is not None:
            place = slice(line * LANES, (line + 1) * LANES)
            lists.append([cols[0][k, :, place] for k in range(K)])
        cols[1](line, reduce_lists(lists))


def store_running(ref):
    def store(*at):
        *place, values = at
        first = place[-1] if len(place) > 1 else place[0] * LANES
        for k in range(K):
            ref[k, :, first : first + LANES] = values[k]

    return store


def first_kernel(piece, targets, cos_out, inv_src, inv_tgt, rows, cols, work, cos_ref, sem):
    cosine_block(
        [piece], targets, (None, inv_src), (None, inv_tgt), cos_ref,
        (None, store_running(rows)), (None, store_running(cols)), work,
    )
    pltpu.make_async_copy(cos_ref, cos_out, sem).start()
    pltpu.make_async_copy(cos_ref, cos_out, sem).wait()


def next_kernel(piece, targets, inv_tgt, cols_in, cos_ref, inv_src, rows, cols, work):
    cosine_block(
        [piece], targets, (None, inv_src), (inv_tgt, None), cos_ref,
        (None, store_running(rows)), (cols_in, store_running(cols)), work,
    )


def last_kernel(pieces, targets, inv_src, rows_in, cols_in, cos_ref, row_ref, col_ref, work, inv_tgt):
    lines = cols_in.shape[2] // LANES
    slot = rows_in[0].shape[2] // LANES

    def store_row(b, n, values):
        store_lists(row_ref, fold_sublanes(values), b * slot + n // LANES)

    def store_col(line, values):
        store_lists(col_ref, fold_sublanes(values), lines + line)

    cosine_block(
        pieces, targets, (inv_src, None), (None, inv_tgt), cos_ref,
        (rows_in, store_row), (None, store_col), work,
    )
    for line in range(lines):
        place = slice(line * LANES, (line + 1) * LANES)
        store_lists(col_ref, fold_sublanes([cols_in[k, :, place] for k in range(K)]), line)


def flipped(ref, k, unit):
    step = unit // LANES
    values = ref[k]
    if step:
        lines = [line ^ step for line in range(ref.shape[1])]
        values = jnp.concatenate([ref[k, line : line + 1, :] for line in lines], axis=0)
    lane = lax.broadcasted_iota(jnp.int32, values.shape, 1)
    for bit in bits_below(LANES):
        if unit & bit:
            up, down = pltpu.roll(values, LANES - bit, 1), pltpu.roll(values, bit, 1)
            values = jnp.where((lane & bit) == 0, up, down)
    return values


def merged(mine, arrived, unit):
    return merge_lists([mine[k] for k in range(K)], [flipped(arrived, k, unit) for k in range(K)])


def merge_kernel(unit, mine, arrived, out_ref):
    for k, values in enumerate(merged(mine, arrived, unit)):
        out_ref[k] = values


def spread(ref, line):
    return jnp.broadcast_to(ref[line : line + 1, :] * 0.5, (LANES, LANES))


def margin_lists(early, late, first, fwd_ref, bwd_down, out_ref):
    n_early, n_late = early.shape[0], late.shape[0]
    for s in range(0, early.shape[1], LANES):
        fwd = spread(fwd_ref, (first + s) // LANES)
        lists = []
        for t in range(0, n_early + n_late, LANES):
            if t < n_early:
                tile = early[t : t + LANES, s : s + LANES]
            else:
                tile = late[t - n_early : t - n_early + LANES, first + s : first + s + LANES]
            lists.append(fold(tile / (fwd + bwd_down[t : t + LANES, :])))
        store_lists(out_ref, fold_sublanes(reduce_lists(lists)), s // LANES)


def sent_kernel(unit, early, late, rows, cols, *outs):
    *lists, fwd_ref, bwd_ref, bwd_down = outs
    fwd_ref[...] = sum(merged(*rows, 0)) / K
    bwd_ref[...] = sum(merged(*cols, unit)) / K
    for line in range(bwd_ref.shape[0]):
        bwd_down[line * LANES : (line + 1) * LANES, :] = spread(bwd_ref, line).T
    for n, out_ref in enumerate(lists):
        margin_lists(early[n], late, (n + 1) * early[n].shape[1], fwd_ref, bwd_down, out_ref)


def kept_kernel(first, late, fwd_ref, bwd_down, out_ref, held, sem):
    arriving = pltpu.make_async_copy(first, held, sem)
    arriving.start()
    arriving.wait()
    margin_lists(held, late, 0, fwd_ref, bwd_down, out_ref)


def place_kernel(near, far, lines, known, out_ref):
    at = lax.axis_index("src")
    for b in range(near):
        for a in range(far):
            for c in range(2):
                slot = (b * far + a) * 2 + c
                first = (at ^ ((a * near + b) * 2 + c)) * lines
                out_ref[pl.ds(first, lines), :] = known[slot * lines : (slot + 1) * lines, :]


def prepare_kernel(source, target, source_out, target_out, sems):
    copies = [
        pltpu.make_async_copy(source, source_out, sems.at[0]),
        pltpu.make_async_copy(target, target_out, sems.at[1]),
    ]
    for copy in copies:
        copy.start()
    for copy in copies:
        copy.wait()


def call(kernel, args, out_shapes, scratch=(), flops=0, hbm_in=(), hbm_out=(), sems=0):
    vmem = pl.BlockSpec(memory_space=pltpu.VMEM)
    hbm = pl.BlockSpec(memory_space=pltpu.HBM)
    in_specs = [
        jax.tree.map(lambda _: hbm if n in hbm_in else vmem, arg) for n, arg in enumerate(args)
    ]
    return pl.pallas_call(
        kernel,
        out_shape=tuple(jax.ShapeDtypeStruct(shape, jnp.float32) for shape in out_shapes),
        in_specs=in_specs,
        out_specs=tuple(hbm if n in hbm_out else vmem for n in range(len(out_shapes))),
        scratch_shapes=[pltpu.VMEM(shape, jnp.float32) for shape in scratch]
        + [pltpu.SemaphoreType.DMA] * sems,
        compiler_params=pltpu.CompilerParams(vmem_limit_bytes=16 << 20),
        cost_estimate=pl.CostEstimate(flops=flops, transcendentals=0, bytes_accessed=0),
    )(*args)


def merge_arrays(one, other, unit=0):
    return call(functools.partial(merge_kernel, unit), (one, other), [one.shape])[0]


def prepare(source, target):
    return pl.pallas_call(
        prepare_kernel,
        out_shape=tuple(jax.ShapeDtypeStruct(a.shape, a.dtype) for a in (source, target)),
        in_specs=[pl.BlockSpec(memory_space=pl.ANY)] * 2,
        out_specs=(pl.BlockSpec(memory_space=pltpu.VMEM),) * 2,
        scratch_shapes=[pltpu.SemaphoreType.DMA((2,))],
        compiler_params=pltpu.CompilerParams(vmem_limit_bytes=4 << 20),
        name="prepare",
    )(source, target)


def xor_pairs(size, mask):
    return [(i, i ^ mask) for i in range(size)]


def flip(array, axis, mask):
    shape = array.shape
    split = shape[:axis] + (shape[axis] // (2 * mask), 2, mask) + shape[axis + 1 :]
    parts = array.reshape(split)
    low = lax.slice_in_dim(parts, 0, 1, axis=axis + 1)
    high = lax.slice_in_dim(parts, 1, 2, axis=axis + 1)
    return jnp.concatenate([high, low], axis=axis + 1).reshape(shape)


def flip_where(bit, array, axis, mask):
    return jnp.where(bit != 0, flip(array, axis, mask), array)


def solution(mesh):
    n_src, n_tgt = mesh.shape["src"], mesh.shape["tgt"]
    near = 1 << (((n_src // 2).bit_length() - 1) // 2)
    far = n_src // 2 // near

    def over_src(array, mask):
        return lax.ppermute(array, "src", xor_pairs(n_src, mask))

    def over_tgt(array, mask):
        return lax.ppermute(array, "tgt", xor_pairs(n_tgt, mask))

    def over_both(array, src_mask, tgt_mask):
        pairs = xor_pairs(n_src * n_tgt, src_mask * n_tgt + tgt_mask)
        return lax.ppermute(array, ("src", "tgt"), pairs)

    def local(source, target):
        rows, _ = source.shape
        t_rows, width = target.shape
        own_source, own_target = prepare(source, target)
        pieces = [[None] * n_tgt for _ in range(near)]
        square = (near, n_tgt) == (2, 2)
        held = [own_target] + [None] * (far - 1)
        for t in range(n_tgt):
            for b in range(near):
                if (b, t) == (0, 0):
                    pieces[b][t] = [own_source]
                elif not (square and b and t):
                    pieces[b][t] = [over_both(source, 2 * b, t)]
        for a in range(1, far):
            if (far, a) != (4, 3):
                held[a] = over_src(target, 2 * near * a)
        if square:
            half = rows // 2
            low = over_src(pieces[0][1][0][:half], 2)
            high = over_tgt(pieces[1][0][0][half:], 1)
            pieces[1][1] = [low, high]
        if far == 4:
            held[3] = over_src(held[2], 2 * near)
        pairs = []
        for a in range(far):
            pairs.append([held[a], over_src(held[a] if a else target, 1)])
        n_late = max(1, LANES // (2 * t_rows))
        early = sum(pairs[: far - n_late], [])
        late = sum(pairs[far - n_late :], [])
        e_rows, l_rows = len(early) * t_rows, len(late) * t_rows
        block_src, block_tgt = near * rows, 2 * far * t_rows
        src_lines, tgt_lines = block_src // LANES, block_tgt // LANES
        running = (K, SUBLANES, rows), (K, SUBLANES, e_rows)
        cos, inv, inv_tgt, row_run, cols = call(
            first_kernel, (pieces[0], early),
            [(e_rows, rows), (SUBLANES, rows), (e_rows, LANES), *running],
            [(e_rows, rows)] * 2, 2 * e_rows * rows * width, hbm_out=(0,), sems=1,
        )
        cosines, inverses, row_runs = [cos], [inv], [row_run]
        for b in range(1, near):
            cos, inv, row_run, cols = call(
                next_kernel, (pieces[b], early, inv_tgt, cols),
                [(e_rows, rows), (SUBLANES, rows), *running],
                [(e_rows, rows)], 2 * e_rows * rows * width,
            )
            cosines.append(cos)
            inverses.append(inv)
            row_runs.append(row_run)
        cos_late, row_best, col_best = call(
            last_kernel, (pieces, late, inverses, row_runs, cols),
            [(l_rows, block_src), (K, src_lines, LANES), (K, tgt_lines, LANES)],
            [(l_rows, block_src), (l_rows, LANES)], 2 * l_rows * block_src * width,
        )

        arrived = over_src(col_best, 1)
        col_best = merge_arrays(col_best, arrived, t_rows)
        for bit in bits_below(near):
            arrived = over_src(row_best, 2 * bit)
            row_best = merge_arrays(row_best, arrived, bit * rows)
        for bit in bits_below(n_tgt):
            arrived = over_tgt(row_best, bit)
            if 2 * bit < n_tgt:
                row_best = merge_arrays(row_best, arrived)
        row_pair = [row_best, arrived]
        for bit in bits_below(far):
            arrived = over_src(col_best, 2 * near * bit + 1)
            if 2 * bit < far:
                col_best = merge_arrays(col_best, arrived, (2 * bit + 1) * t_rows)
        col_pair = [col_best, arrived]
        lines = rows // LANES
        *sent, fwd, bwd, bwd_down = call(
            functools.partial(sent_kernel, (far + 1) * t_rows),
            (cosines[1:], cos_late, row_pair, col_pair),
            [(K, lines, LANES)] * (near - 1)
            + [(src_lines, LANES), (tgt_lines, LANES), (block_tgt, LANES)],
        )
        (own,) = call(
            kept_kernel, (cosines[0], cos_late, fwd, bwd_down),
            [(K, lines, LANES)], [cosines[0].shape], 2 * block_tgt * rows * K, hbm_in=(0,), sems=1,
        )
        best = dict(enumerate([own, *sent]))
        known = bwd.reshape(1, tgt_lines, LANES)
        for bit in bits_below(near):
            send = [slot for slot in best if slot & bit]
            keep = [slot for slot in best if not slot & bit]
            lists = jnp.concatenate([best[slot] for slot in send], axis=1)
            split = lists.size // LANES
            payload = jnp.concatenate(
                [lists.reshape(split, LANES), known.reshape(-1, LANES)], axis=0
            )
            arrived = over_src(payload, 2 * bit)
            mine = jnp.concatenate([best[slot] for slot in keep], axis=1)
            mine = merge_arrays(mine, arrived[:split].reshape(mine.shape))
            best = {slot: mine[:, n * lines : (n + 1) * lines] for n, slot in enumerate(keep)}
            known = jnp.concatenate([known, arrived[split:].reshape(known.shape)], axis=0)
        best = best[0]
        for bit in bits_below(n_tgt):
            best = merge_arrays(best, over_tgt(best, bit))
        if t_rows % LANES == 0:
            (bwd_mean,) = call(
                functools.partial(place_kernel, near, far, t_rows // LANES),
                (known.reshape(-1, LANES),), [(near * tgt_lines, LANES)],
            )
            return fwd[: rows // LANES].reshape(-1), bwd_mean.reshape(-1), best.reshape(K, rows)
        at = lax.axis_index("src")
        known = known.reshape(near, far, 2, t_rows)
        for axis, size, unit in ((0, near, 2), (1, far, 2 * near), (2, 2, 1)):
            for bit in bits_below(size):
                known = flip_where(at & (unit * bit), known, axis, bit)
        bwd_mean = known.transpose(1, 0, 2, 3).reshape(-1)
        return fwd[: rows // LANES].reshape(-1), bwd_mean, best.reshape(K, rows)

    in_specs = (P("src", "tgt"), P(("tgt", "src"), None))
    out_specs = (P("src"), P("tgt"), P(None, "src"))

    return jax.shard_map(local, mesh=mesh, in_specs=in_specs, out_specs=out_specs, check_vma=False)
```
